128 devices in a mesh: phi: 16 (over y_hi, z, core), gz: 8 (over y_lo, x).
Axes of the slice: x: 4, y: 4 (y_hi: 2, y_lo: 2; y = y_hi * 2 + y_lo), z: 4, core: 2. Of those that a mesh axis runs over, the one named last changes fastest.
Arguments:
- electric_radial: float32 [192, 128, 2048], P('gz', None, 'phi'), may hold values from -6 to 6
- electric_azimuth: float32 [192, 128, 2048], P('gz', None, 'phi'), may hold values from -6 to 6
- electric_height: float32 [192, 128, 2048], P('gz', None, 'phi'), may hold values from -6 to 6
- magnetic_radial: float32 [192, 128, 2048], P('gz', None, 'phi'), may hold values from -6 to 6
- magnetic_azimuth: float32 [192, 128, 2048], P('gz', None, 'phi'), may hold values from -6 to 6
- magnetic_height: float32 [192, 128, 2048], P('gz', None, 'phi'), may hold values from -6 to 6
- material: int32 [192, 128, 2048], P('gz', None, 'phi'), may hold values from 0 to 7
- permittivity: float32 [8], replicated, may hold values from 1 to 10
- conductivity: float32 [8], replicated, may hold values from 0.05 to 5
- mode_cutoff: int32 [32], replicated, may hold values from 1 to 127, as said below
Outputs:
- updated_electric_radial: float32 [192, 128, 2048], P('gz', None, 'phi')
- updated_electric_azimuth: float32 [192, 128, 2048], P('gz', None, 'phi')
- updated_electric_height: float32 [192, 128, 2048], P('gz', None, 'phi')
- updated_magnetic_radial: float32 [192, 128, 2048], P('gz', None, 'phi')
- updated_magnetic_azimuth: float32 [192, 128, 2048], P('gz', None, 'phi')
- updated_magnetic_height: float32 [192, 128, 2048], P('gz', None, 'phi')
The draws below stay inside these ranges and needn't reach their ends.
Inputs may be any that keep to these rules, and one draw needn't show every extreme that they name: `mode_cutoff`: cutoffs never fall from one filtered row to the next outward, and the outermost filtered row's cutoff is 127.
All inputs are finite; a program needn't handle non-finite values.
Results may differ from the reference program's by a relative error of at most 0.00005.
Values sent between devices are 32-bit elements; how exact they have to be, the bound alone decides.
A program may use at most 128 MiB of HBM per device.

```python
import math
import jax
import jax.numpy as jnp
from jax import lax

NPHI = 2048
KMAX = 128
NF = 32
NMAT = 8
NR = 128
NZ = 192


def draw_mode_cutoff(key, part):
    raw_values = jax.random.randint(key, (NF,), 1, KMAX)
    ordered = jnp.sort(raw_values)
    return ordered.at[NF - 1].set(KMAX - 1).astype(jnp.int32)


def touch_ends(entries, own_key, least, high):
    dims = entries.shape
    index_at = [jax.random.randint(jax.random.fold_in(own_key, axis), (), 0, dims[axis]) for axis in range(len(dims))]
    entries = entries.at[tuple(index_at)].set(least)
    longest = dims.index(max(dims))
    index_at[longest] = (index_at[longest] + 1) % dims[longest]
    return entries.at[tuple(index_at)].set(high)


def steps_of(own_key, shape, shards, smallest, high):
    loudness = 1.0
    for axis_at, parts in shards:
        heights = jax.random.uniform(jax.random.fold_in(jax.random.fold_in(own_key, 6), axis_at), (parts,), jnp.float32, smallest / len(shards), high / len(shards))
        loudness = loudness * jnp.repeat(jnp.exp(heights), shape[axis_at] // parts).reshape((-1,) + (1,) * (len(shape) - 1 - axis_at))
    return loudness


def gaussian(rng, dims, spread, most, shards=(), kind=jnp.bfloat16):
    drawn = spread * jax.random.normal(rng, dims, jnp.float32)
    if shards:
        drawn = drawn * steps_of(rng, dims, shards, -0.22, 0.18)
    return jnp.clip(drawn, -most, most).astype(kind)


def setup_inputs(seed: int = 0) -> dict:
    arg_keys = jax.random.split(jax.random.key(seed), 11)
    return {
        "electric_radial": gaussian(arg_keys[0], (NZ, NR, NPHI), 1.0, 6.0, ((0, 8), (2, 16)), jnp.float32),
        "electric_azimuth": gaussian(arg_keys[1], (NZ, NR, NPHI), 1.0, 6.0, ((0, 8), (2, 16)), jnp.float32),
        "electric_height": gaussian(arg_keys[2], (NZ, NR, NPHI), 1.0, 6.0, ((0, 8), (2, 16)), jnp.float32),
        "magnetic_radial": gaussian(arg_keys[3], (NZ, NR, NPHI), 1.0, 6.0, ((0, 8), (2, 16)), jnp.float32),
        "magnetic_azimuth": gaussian(arg_keys[4], (NZ, NR, NPHI), 1.0, 6.0, ((0, 8), (2, 16)), jnp.float32),
        "magnetic_height": gaussian(arg_keys[5], (NZ, NR, NPHI), 1.0, 6.0, ((0, 8), (2, 16)), jnp.float32),
        "material": touch_ends(jax.random.randint(arg_keys[6], (NZ, NR, NPHI), 0, NMAT), jax.random.fold_in(arg_keys[6], 1), 0, NMAT - 1).astype(jnp.int32),
        "permittivity": jnp.clip(jnp.exp(jax.random.uniform(arg_keys[7], (NMAT,), jnp.float32, math.log(1.0), math.log(10.0))), 1.0, 10.0),
        "conductivity": jnp.clip(jnp.exp(jax.random.uniform(arg_keys[8], (NMAT,), jnp.float32, math.log(0.05), math.log(5.0))), 0.05, 5.0),
        "mode_cutoff": draw_mode_cutoff(jax.random.fold_in(arg_keys[10], 71), 0),
    }


inner_radius = 64.0
time_step = 0.2


def forward_step(values, along, cyclic):
    if cyclic:
        return jnp.roll(values, -1, along) - values
    length = values.shape[along]
    zero_slab = jnp.zeros_like(lax.slice_in_dim(values, 0, 1, axis=along))
    return jnp.concatenate([lax.slice_in_dim(values, 1, length, axis=along), zero_slab], along) - values


def backward_step(values, along, cyclic):
    if cyclic:
        return values - jnp.roll(values, 1, along)
    length = values.shape[along]
    zero_slab = jnp.zeros_like(lax.slice_in_dim(values, 0, 1, axis=along))
    return values - jnp.concatenate([zero_slab, lax.slice_in_dim(values, 0, length - 1, axis=along)], along)


def cycle_filter(values, mode_cutoff):
    inner_rows = values[:, :NF, :]
    spectrum = jnp.fft.rfft(inner_rows, axis=2)
    mode_index = jnp.arange(NPHI // 2 + 1, dtype=jnp.int32)
    kept = mode_index[None, :] <= mode_cutoff[:, None]
    filtered = jnp.fft.irfft(jnp.where(kept[None], spectrum, 0.0), n=NPHI, axis=2).astype(values.dtype)
    return jnp.concatenate([filtered, values[:, NF:, :]], axis=1)


def reference(electric_radial, electric_azimuth, electric_height, magnetic_radial, magnetic_azimuth, magnetic_height, material, permittivity, conductivity, mode_cutoff):
    node_radius = (inner_radius + jnp.arange(NR, dtype=jnp.float32))[None, :, None]
    center_radius = node_radius + 0.5
    angle_step = 2.0 * math.pi / NPHI
    radial_half = magnetic_radial - time_step * (forward_step(electric_height, 2, True) / (node_radius * angle_step) - forward_step(electric_azimuth, 0, False))
    azimuth_half = magnetic_azimuth - time_step * (forward_step(electric_radial, 0, False) - forward_step(electric_height, 1, False))
    height_half = magnetic_height - time_step * (forward_step(node_radius * electric_azimuth, 1, False) / center_radius - forward_step(electric_radial, 2, True) / (center_radius * angle_step))
    new_hr = cycle_filter(radial_half, mode_cutoff)
    new_hp = cycle_filter(azimuth_half, mode_cutoff)
    new_hz = cycle_filter(height_half, mode_cutoff)
    epsilon = permittivity[material]
    losses = conductivity[material] * time_step / (2.0 * epsilon)
    keep_factor = (1.0 - losses) / (1.0 + losses)
    drive_factor = time_step / (epsilon * (1.0 + losses))
    radial_next = keep_factor * electric_radial + drive_factor * (backward_step(new_hz, 2, True) / (center_radius * angle_step) - backward_step(new_hp, 0, False))
    azimuth_next = keep_factor * electric_azimuth + drive_factor * (backward_step(new_hr, 0, False) - backward_step(new_hp, 1, False))
    height_next = keep_factor * electric_height + drive_factor * (backward_step(center_radius * new_hp, 1, False) / node_radius - backward_step(new_hr, 2, True) / (node_radius * angle_step))
    return (cycle_filter(radial_next, mode_cutoff), cycle_filter(azimuth_next, mode_cutoff), cycle_filter(height_next, mode_cutoff), new_hr, new_hp, new_hz)
```

```python
import functools
import math

import jax
import jax.numpy as jnp
import numpy as np
from jax import lax
from jax.experimental import pallas as pl
from jax.experimental.pallas import tpu as pltpu
from jax.sharding import PartitionSpec as P

KMAX = 128
NF = 32
NMAT = 8
NPHI = 2048
NR = 128
LAYERS = 24
WIDTH = 128
CHUNKS = 3
PER_CHUNK = 8
HALF = 4
HALO_R = 32

inner_radius = 64.0
dt = 0.2
dphi = 2.0 * math.pi / NPHI
MESH = pl.DeviceIdType.MESH
F32 = jnp.float32
BF16 = jnp.bfloat16

C_DT_RN, C_UP, C_HERE, C_DT_RC, C_RC, C_KEEP_PREV, C_P, C_Q, C_RN = range(9)
ST_A, ST_1A, ST_1B, ST_2A, ST_2B, ST_C, ST_3A, ST_3B, ST_4A, ST_4B, ST_Z = range(11)
NSTAGE = 13
B_P1I, B_P1O, B_ER, B_EA, B_P2, B_HI, B_HO = range(7)


def basis_tables():
    j = np.arange(WIDTH, dtype=np.float64)[:, None]
    m = np.arange(KMAX, dtype=np.float64)[None, :]
    a = 2.0 * np.pi * j * m / NPHI
    b = 2.0 * np.pi * (j - 1.0) * m / NPHI
    base = np.stack([np.cos(a), np.sin(a), np.cos(a) - np.cos(b), np.sin(a) - np.sin(b)])
    turn = 2.0 * np.pi * ((np.arange(16)[:, None] * WIDTH * np.arange(KMAX)[None, :]) % NPHI) / NPHI
    phase = np.stack([np.cos(turn), np.sin(turn)])
    return base.astype(np.float32), phase.astype(np.float32)


def split(x):
    hi = x.astype(BF16)
    lo = (x - hi.astype(F32)).astype(BF16)
    return hi, lo


def dot3(x, b_hi, b_lo):
    hi, lo = split(x)
    out = jnp.dot(hi, b_hi, preferred_element_type=F32)
    out += jnp.dot(lo, b_hi, preferred_element_type=F32)
    out += jnp.dot(hi, b_lo, preferred_element_type=F32)
    return out


def kernel(
    er_h, ea_h, eh_h, mr_h, mp_h, mz_h, mat_h, perm, cond, cut, base, phase,
    o_er, o_ea, o_eh, o_hr, o_hp, o_hz,
    er, ea, eh, mr, mp, mz, mat,
    coef, ktab, wts, fwd, inv,
    p1s, p1r, p2s, p2r,
    g, ra, s, r1, r2, u, rc_buf, t, v, v2, hf, ho, ki,
    in_sem, send, recv, bsend, brecv,
):
    phi = lax.axis_index("phi")
    gz = lax.axis_index("gz")
    q = phi % 2
    z = (phi // 2) % 4
    hi_bit = z // 2
    low_bit = z % 2
    gray = (hi_bit + low_bit) % 2
    sib = phi + 1 - 2 * q
    chip_z1 = z + 1 - 2 * low_bit
    chip_z3 = 3 - z
    top_y = phi // 8
    dev_z1 = top_y * 8 + chip_z1 * 2 + q
    dev_z3 = top_y * 8 + chip_z3 * 2 + q
    dev_y = (phi + 8) % 16
    nxt = (phi + 1) % 16
    prv = (phi + 15) % 16
    up = (gz + 1) % 8
    down = (gz + 7) % 8
    f1, f2 = gray, hi_bit
    g1, g2 = hi_bit, gray

    lane = lax.broadcasted_iota(jnp.int32, (1, 128), 1)

    loads = []
    RI = 40
    for n, (src, dst, k) in enumerate(
        [(eh_h, eh, LAYERS), (er_h, er, LAYERS), (ea_h, ea, LAYERS), (mr_h, mr, 0), (mp_h, mp, 0), (mz_h, mz, 0), (mat_h, mat, 0)]
    ):
        d = dst.at[0:LAYERS] if k else dst
        inner = pltpu.make_async_copy(src.at[:, 0:RI], d.at[:, 0:RI], in_sem.at[2 * n])
        outer = pltpu.make_async_copy(src.at[:, RI:NR], d.at[:, RI:NR], in_sem.at[2 * n + 1])
        loads.append((inner, outer))
    for inner, _ in loads:
        inner.start()
    for _, outer in loads:
        outer.start()

    barrier = pltpu.get_barrier_semaphore()
    for d in (sib, dev_z1, dev_z3, dev_y, nxt, prv):
        pl.semaphore_signal(barrier, inc=1, device_id={"phi": d}, device_id_type=MESH)
    for d in (up, down):
        pl.semaphore_signal(barrier, inc=1, device_id={"gz": d}, device_id_type=MESH)

    row = lax.broadcasted_iota(jnp.int32, (NR, 128), 0)
    rn = inner_radius + row.astype(F32)
    rc = rn + 0.5
    inv_rn = 1.0 / rn
    inv_rc = 1.0 / rc
    first = row == 0
    coef[C_DT_RN] = (dt / dphi) * inv_rn
    coef[C_UP] = dt * (rn + 1.0) * inv_rc
    coef[C_HERE] = dt * rn * inv_rc
    coef[C_DT_RC] = (dt / dphi) * inv_rc
    coef[C_RC] = (1.0 / dphi) * inv_rc
    coef[C_KEEP_PREV] = jnp.where(first, 0.0, 1.0)
    coef[C_P] = rc * inv_rn
    coef[C_Q] = jnp.where(first, 0.0, (rc - 1.0) * inv_rn)
    coef[C_RN] = (1.0 / dphi) * inv_rn

    for number in range(NMAT):
        eps = jnp.full((8, 128), perm[number], F32)
        sig = jnp.full((8, 128), cond[number], F32)
        loss = sig * dt / (2.0 * eps)
        ktab[0, number] = (1.0 - loss) / (1.0 + loss)
        ktab[1, number] = dt / (eps * (1.0 + loss))

    mode = lax.broadcasted_iota(jnp.int32, (NF, 128), 1)
    wrow = lax.broadcasted_iota(jnp.int32, (NF, 128), 0)
    cuts = jnp.zeros((NF, 128), jnp.int32)
    for number in range(NF):
        cuts = jnp.where(wrow == number, cut[number], cuts)
    weight = jnp.where(mode == 0, 1.0 / NPHI, 2.0 / NPHI)
    weight = jnp.where(mode <= cuts, weight, 0.0)
    wts[:, 0:128] = weight
    wts[:, 128:256] = weight

    for place, who in ((0, phi), (1, sib)):
        pc = phase[0, pl.ds(who, 1), :]
        ps = phase[1, pl.ds(who, 1), :]
        cosb = base[0] * pc - base[1] * ps
        sinb = base[1] * pc + base[0] * ps
        dcos = base[2] * pc - base[3] * ps
        dsin = base[3] * pc + base[2] * ps
        lo_row = place * 128
        for part, m in ((0, cosb), (1, sinb)):
            h, l = split(m)
            fwd[0, lo_row : lo_row + 128, part * 128 : part * 128 + 128] = h
            fwd[1, lo_row : lo_row + 128, part * 128 : part * 128 + 128] = l
        for kind, (mc, ms) in ((0, (cosb, sinb)), (1, (dcos, dsin))):
            col = kind * 256 + place * 128
            for part, m in ((0, mc), (1, ms)):
                h, l = split(m.T)
                inv[0, part * 128 : part * 128 + 128, col : col + 128] = h
                inv[1, part * 128 : part * 128 + 128, col : col + 128] = l

    def clear(k, _):
        eh[k, NR : NR + 8] = jnp.zeros((8, 128), F32)
        ea[k, NR : NR + 8] = jnp.zeros((8, 128), F32)
        return 0

    lax.fori_loop(0, LAYERS, clear, 0)
    p1s[...] = jnp.zeros_like(p1s)
    p2s[...] = jnp.zeros_like(p2s)

    pl.semaphore_wait(barrier, 8)

    def border(src, dst, n, dev):
        return pltpu.make_async_remote_copy(
            src_ref=src, dst_ref=dst, send_sem=bsend.at[n], recv_sem=brecv.at[n],
            device_id=dev, device_id_type=MESH,
        )

    b_er = border(er_h.at[0], er.at[LAYERS], B_ER, {"gz": down})
    b_ea = border(ea_h.at[0], ea.at[LAYERS, 0:NR], B_EA, {"gz": down})
    b_p1i = border(p1s.at[0:NF], p1r.at[0:NF], B_P1I, {"phi": prv})
    b_p1o = border(p1s.at[NF:NR], p1r.at[NF:NR], B_P1O, {"phi": prv})
    b_p2 = border(p2s, p2r, B_P2, {"phi": nxt})
    b_hi = border(hf.at[LAYERS, 0:2], hf.at[0, 0:2], B_HI, {"gz": up})
    b_ho = border(ho.at[LAYERS, :, 8:104], ho.at[0, :, 8:104], B_HO, {"gz": up})

    b_er.start()
    b_ea.start()

    def pack_first(lo, hi):
        def body(k, _):
            a = pltpu.roll(eh[k, lo:hi], k, 1)
            b = pltpu.roll(er[k, lo:hi], HALO_R + k, 1)
            p1s[lo:hi] = jnp.where(lane == k, a, jnp.where(lane == HALO_R + k, b, p1s[lo:hi]))
            return 0

        lax.fori_loop(0, LAYERS, body, 0)

    loads[0][0].wait()
    loads[1][0].wait()
    pack_first(0, NF)
    b_p1i.start()
    for n in range(2, 6):
        loads[n][0].wait()
    b_er.wait_recv()
    b_ea.wait_recv()
    above = jnp.where(gz == 7, 0.0, 1.0)
    er[LAYERS] = er[LAYERS] * above
    ea[LAYERS, 0:NR] = ea[LAYERS, 0:NR] * above
    b_p1i.wait_recv()

    def magnetic(k, lo, hi):
        def ahead(x, n):
            return jnp.where(lane == 127, pltpu.roll(p1r[lo:hi], 127 - n, 1), pltpu.roll(x, 127, 1)) - x

        e_h = eh[k, lo:hi]
        e_r = er[k, lo:hi]
        e_a = ea[k, lo:hi]
        hr = mr[k, lo:hi] - coef[C_DT_RN, lo:hi] * ahead(e_h, k) + dt * (ea[k + 1, lo:hi] - e_a)
        hp = mp[k, lo:hi] - dt * ((er[k + 1, lo:hi] - e_r) - (eh[k, lo + 1 : hi + 1] - e_h))
        hz = (
            mz[k, lo:hi]
            - (coef[C_UP, lo:hi] * ea[k, lo + 1 : hi + 1] - coef[C_HERE, lo:hi] * e_a)
            + coef[C_DT_RC, lo:hi] * ahead(e_r, HALO_R + k)
        )
        return hr, hp, hz

    def factors(k, lo, hi):
        kind = mat[k, lo:hi]
        keep = jnp.broadcast_to(ktab[0, 0, 0:1], kind.shape)
        drive = jnp.broadcast_to(ktab[1, 0, 0:1], kind.shape)
        for number in range(1, NMAT):
            here = kind == number
            keep = jnp.where(here, ktab[0, number, 0:1], keep)
            drive = jnp.where(here, ktab[1, number, 0:1], drive)
        return keep, drive

    def move(f, c, stage, src, dst, dev):
        n = f * CHUNKS + c
        return pltpu.make_async_remote_copy(
            src_ref=src, dst_ref=dst, send_sem=send.at[n, stage], recv_sem=recv.at[n, stage],
            device_id={"phi": dev}, device_id_type=MESH,
        )

    def d_a(f, c):
        return [move(f, c, ST_A, g.at[f, pl.ds(PER_CHUNK * c + HALF * (1 - q), HALF)], ra.at[f, c], sib)]

    def d_1(f, c):
        return [
            move(f, c, ST_1A, s.at[f, c, pl.ds(2 * (1 - f1), 2), :, 0:16], r1.at[f, c, 0], dev_z1),
            move(f, c, ST_1B, s.at[f, c, pl.ds(2 * (1 - g1), 2), :, 16:32], r1.at[f, c, 1], dev_z3),
        ]

    def d_2(f, c):
        return [
            move(f, c, ST_2A, s.at[f, c, 2 * f1 + 1 - f2, :, 0:16], r2.at[f, c, 0], dev_z3),
            move(f, c, ST_2B, s.at[f, c, 2 * g1 + 1 - g2, :, 16:32], r2.at[f, c, 1], dev_z1),
        ]

    def d_c(f, c):
        return [move(f, c, ST_C, u.at[f, c], rc_buf.at[f, c], dev_y)]

    def d_3(f, c):
        a = t.at[f, c, 2 * f1 + f2, :, 0:16]
        b = t.at[f, c, 2 * g1 + g2, :, 16:32]
        return [move(f, c, ST_3A, a, a, dev_z3), move(f, c, ST_3B, b, b, dev_z1)]

    def d_4(f, c):
        a = t.at[f, c, pl.ds(2 * f1, 2), :, 0:16]
        b = t.at[f, c, pl.ds(2 * g1, 2), :, 16:32]
        return [move(f, c, ST_4A, a, a, dev_z1), move(f, c, ST_4B, b, b, dev_z3)]

    def d_z(f, c):
        start = PER_CHUNK * c + HALF * q
        if f == 0:
            return [move(f, c, ST_Z, v.at[c], hf.at[pl.ds(1 + start, HALF)], sib)]
        return [
            move(f, c, ST_Z + n, v2.at[c, n], o.at[pl.ds(start, HALF), 0:NF], sib)
            for n, o in enumerate((o_er, o_ea, o_eh))
        ]

    def go(copies):
        for d in copies:
            d.start()

    def arrived(copies):
        for d in copies:
            d.wait_recv()

    def stage_1(f, c):
        arrived(d_a(f, c))
        own = g[f, pl.ds(PER_CHUNK * c + HALF * q, HALF)].reshape(HALF * 96, 128)
        x = jnp.concatenate([own, ra[f, c].reshape(HALF * 96, 128)], axis=1)
        s[f, c] = dot3(x, fwd[0], fwd[1]).reshape(HALF, 3, NF, 256)
        go(d_1(f, c))

    def stage_2(f, c):
        arrived(d_1(f, c))
        s[f, c, pl.ds(2 * f1, 2), :, 0:16] = s[f, c, pl.ds(2 * f1, 2), :, 0:16] + r1[f, c, 0]
        s[f, c, pl.ds(2 * g1, 2), :, 16:32] = s[f, c, pl.ds(2 * g1, 2), :, 16:32] + r1[f, c, 1]
        go(d_2(f, c))

    def stage_3(f, c):
        arrived(d_2(f, c))
        u[f, c, 0] = s[f, c, 2 * f1 + f2, :, 0:16] + r2[f, c, 0]
        u[f, c, 1] = s[f, c, 2 * g1 + g2, :, 16:32] + r2[f, c, 1]
        go(d_c(f, c))

    def stage_4(f, c):
        arrived(d_c(f, c))
        t[f, c, 2 * f1 + f2, :, 0:16] = (u[f, c, 0] + rc_buf[f, c, 0]) * wts[0:16][None]
        t[f, c, 2 * g1 + g2, :, 16:32] = (u[f, c, 1] + rc_buf[f, c, 1]) * wts[16:32][None]
        go(d_3(f, c))

    def stage_5(f, c):
        arrived(d_3(f, c))
        go(d_4(f, c))

    def stage_6(f, c):
        arrived(d_4(f, c))
        x = t[f, c].reshape(HALF * 96, 256)
        start = PER_CHUNK * c + HALF * q
        value = dot3(x, inv[0, :, 0:256], inv[1, :, 0:256]).reshape(HALF, 3, NF, 256)
        if f == 0:
            slope = dot3(x, inv[0, :, 256:512], inv[1, :, 256:512]).reshape(HALF, 3, NF, 256)
            v[c, :, 0:3] = value[..., 128:256]
            v[c, :, 3] = slope[:, 0, :, 128:256]
            v[c, :, 4] = slope[:, 2, :, 128:256]
            go(d_z(f, c))
            hf[pl.ds(1 + start, HALF), 0:3] = value[..., 0:128]
            hf[pl.ds(1 + start, HALF), 3] = slope[:, 0, :, 0:128]
            hf[pl.ds(1 + start, HALF), 4] = slope[:, 2, :, 0:128]
        else:
            for n in range(3):
                v2[c, n] = value[:, n, :, 128:256]
            go(d_z(f, c))
            for n, o in enumerate((o_er, o_ea, o_eh)):
                o[pl.ds(start, HALF), 0:NF] = value[:, n, :, 0:128]

    def each(stage, f):
        def body(c, _):
            stage(f, c)
            return 0

        lax.fori_loop(0, CHUNKS, body, 0)

    def begin_h(f, c):
        def body(k, _):
            hr, hp, hz = magnetic(k, 0, NF)
            g[0, k, 0] = hr
            g[0, k, 1] = hp
            g[0, k, 2] = hz
            return 0

        lax.fori_loop(PER_CHUNK * c, PER_CHUNK * c + PER_CHUNK, body, 0)
        go(d_a(0, c))

    each(begin_h, 0)
    for n in range(7):
        loads[n][1].wait()
    loads[6][0].wait()
    pack_first(NF, NR)
    b_p1o.start()
    each(stage_1, 0)

    def inner_factors(k, _):
        keep, drive = factors(k, 0, NF)
        ki[k, 0] = keep
        ki[k, 1] = drive
        return 0

    lax.fori_loop(0, LAYERS, inner_factors, 0)
    b_p1o.wait_recv()
    each(stage_2, 0)

    def outer_h(k, _):
        hr, hp, hz = magnetic(k, NF, NR)
        ho[k + 1, 0, 8:104] = hr
        ho[k + 1, 1, 8:104] = hp
        o_hz[k, NF:NR] = hz
        p2s[...] = jnp.where(
            lane == k,
            pltpu.roll(hr, k + 1, 1),
            jnp.where(lane == HALO_R + k, pltpu.roll(hz, HALO_R + k + 1, 1), p2s[...]),
        )
        return 0

    each(stage_3, 0)
    lax.fori_loop(0, LAYERS, outer_h, 0)
    b_p2.start()
    b_ho.start()
    each(stage_4, 0)
    each(stage_5, 0)
    each(stage_6, 0)

    below = jnp.where(gz == 0, 0.0, 1.0)

    def electric_inner(k, _):
        hr, hp, hz = hf[k + 1, 0], hf[k + 1, 1], hf[k + 1, 2]
        keep, drive = ki[k, 0], ki[k, 1]
        back = pltpu.roll(hp, 1, 0)
        g[1, k, 0] = keep * er[k, 0:NF] + drive * (coef[C_RC, 0:NF] * hf[k + 1, 4] - (hp - hf[k, 1]))
        g[1, k, 1] = keep * ea[k, 0:NF] + drive * ((hr - hf[k, 0]) - (hp - coef[C_KEEP_PREV, 0:NF] * back))
        g[1, k, 2] = keep * eh[k, 0:NF] + drive * (
            coef[C_P, 0:NF] * hp - coef[C_Q, 0:NF] * back - coef[C_RN, 0:NF] * hf[k + 1, 3]
        )
        return 0

    def begin_e(c):
        lax.fori_loop(PER_CHUNK * c, PER_CHUNK * c + PER_CHUNK, electric_inner, 0)
        go(d_a(1, c))

    for c in range(CHUNKS):
        arrived(d_z(0, c))
    b_hi.start()
    begin_e(1)
    begin_e(2)
    b_hi.wait_recv()
    hf[0, 0:2] = hf[0, 0:2] * below
    begin_e(0)

    def in_order(stage, f):
        def body(n, _):
            stage(f, (n + 1) % CHUNKS)
            return 0

        lax.fori_loop(0, CHUNKS, body, 0)

    in_order(stage_1, 1)

    def finish_h(k, _):
        o_hr[k, 0:NF] = hf[k + 1, 0]
        o_hp[k, 0:NF] = hf[k + 1, 1]
        o_hz[k, 0:NF] = hf[k + 1, 2]
        ho[k + 1, 1, 0:8] = hf[k + 1, 1, 24:32]
        return 0

    lax.fori_loop(0, LAYERS, finish_h, 0)
    in_order(stage_2, 1)
    b_p2.wait_recv()
    b_ho.wait_recv()
    ho[0, :, 8:104] = ho[0, :, 8:104] * below

    def outer_e(k, _):
        hr, hp = ho[k + 1, 0, 8:104], ho[k + 1, 1, 8:104]
        hz = o_hz[k, NF:NR]
        back = ho[k + 1, 1, 7:103]
        keep, drive = factors(k, NF, NR)

        def behind(x, n):
            return x - jnp.where(lane == 0, pltpu.roll(p2r[...], (128 - n) % 128, 1), pltpu.roll(x, 1, 1))

        o_hr[k, NF:NR] = hr
        o_hp[k, NF:NR] = hp
        o_er[k, NF:NR] = keep * er[k, NF:NR] + drive * (
            coef[C_RC, NF:NR] * behind(hz, HALO_R + k) - (hp - ho[k, 1, 8:104])
        )
        o_ea[k, NF:NR] = keep * ea[k, NF:NR] + drive * ((hr - ho[k, 0, 8:104]) - (hp - back))
        o_eh[k, NF:NR] = keep * eh[k, NF:NR] + drive * (
            coef[C_P, NF:NR] * hp - coef[C_Q, NF:NR] * back - coef[C_RN, NF:NR] * behind(hr, k)
        )
        return 0

    in_order(stage_3, 1)
    lax.fori_loop(0, LAYERS, outer_e, 0)
    in_order(stage_4, 1)
    in_order(stage_5, 1)
    in_order(stage_6, 1)
    for c in range(CHUNKS):
        arrived(d_z(1, c))

    def drained(c, _):
        for f in range(2):
            for kind in (d_a, d_1, d_2, d_c, d_3, d_4, d_z):
                for d in kind(f, c):
                    d.wait_send()
        return 0

    lax.fori_loop(0, CHUNKS, drained, 0)
    for d in (b_er, b_ea, b_p1i, b_p1o, b_p2, b_hi, b_ho):
        d.wait_send()


def local(er, ea, eh, mr, mp, mz, material, permittivity, conductivity, mode_cutoff):
    base, phase = basis_tables()
    field = (LAYERS, NR, WIDTH)
    anywhere = pl.BlockSpec(memory_space=pl.ANY)
    smem = pl.BlockSpec(memory_space=pltpu.SMEM)
    vmem = pl.BlockSpec(memory_space=pltpu.VMEM)

    def scratch(*shape, dtype=F32):
        return pltpu.VMEM(shape, dtype)

    call = pl.pallas_call(
        kernel,
        out_shape=tuple(pltpu.VMEM(field, F32) for _ in range(6)),
        in_specs=[anywhere] * 7 + [smem] * 3 + [vmem] * 2,
        out_specs=tuple([vmem] * 6),
        scratch_shapes=[
            scratch(LAYERS + 1, NR, WIDTH),
            scratch(LAYERS + 1, NR + 8, WIDTH),
            scratch(LAYERS, NR + 8, WIDTH),
            scratch(*field),
            scratch(*field),
            scratch(*field),
            scratch(*field, dtype=jnp.int32),
            scratch(9, NR, 128),
            scratch(2, NMAT, 8, 128),
            scratch(NF, 256),
            scratch(2, 256, 256, dtype=BF16),
            scratch(2, 256, 512, dtype=BF16),
            scratch(NR, 128),
            scratch(NR, 128),
            scratch(NR - NF, 128),
            scratch(NR - NF, 128),
            scratch(2, LAYERS, 3, NF, 128),
            scratch(2, CHUNKS, HALF, 3, NF, 128),
            scratch(2, CHUNKS, HALF, 3, NF, 256),
            scratch(2, CHUNKS, 2, 2, 3, 16, 256),
            scratch(2, CHUNKS, 2, 3, 16, 256),
            scratch(2, CHUNKS, 2, 3, 16, 256),
            scratch(2, CHUNKS, 2, 3, 16, 256),
            scratch(2, CHUNKS, HALF, 3, NF, 256),
            scratch(CHUNKS, HALF, 5, NF, 128),
            scratch(CHUNKS, 3, HALF, NF, 128),
            scratch(LAYERS + 1, 5, NF, 128),
            scratch(LAYERS + 1, 2, 104, 128),
            scratch(LAYERS, 2, NF, 128),
            pltpu.SemaphoreType.DMA((14,)),
            pltpu.SemaphoreType.DMA((2 * CHUNKS, NSTAGE)),
            pltpu.SemaphoreType.DMA((2 * CHUNKS, NSTAGE)),
            pltpu.SemaphoreType.DMA((7,)),
            pltpu.SemaphoreType.DMA((7,)),
        ],
        compiler_params=pltpu.CompilerParams(
            collective_id=0, has_side_effects=True, vmem_limit_bytes=44 * 1024 * 1024
        ),
        name="yee_step",
    )
    return call(
        er, ea, eh, mr, mp, mz, material, permittivity, conductivity, mode_cutoff,
        jnp.asarray(base), jnp.asarray(phase),
    )


def solution(mesh):
    field = P("gz", None, "phi")
    return jax.shard_map(
        local,
        mesh=mesh,
        in_specs=(field,) * 7 + (P(),) * 3,
        out_specs=(field,) * 6,
        check_vma=False,
    )
```

```python
import math

import jax
import jax.numpy as jnp
import numpy as np
from jax import lax
from jax.experimental import pallas as pl
from jax.experimental.pallas import tpu as pltpu
from jax.sharding import PartitionSpec as P

KMAX = 128
NF = 32
NMAT = 8
NPHI = 2048
NR = 128
OUT = NR - NF
LAYERS = 24
WIDTH = 128
CHUNKS = 3
PER_CHUNK = 8
PAIRS = LAYERS // 2
HALO_R = 32

inner_radius = 64.0
dt = 0.2
dphi = 2.0 * math.pi / NPHI
MESH = pl.DeviceIdType.MESH
F32 = jnp.float32
BF16 = jnp.bfloat16

C_DT_RN, C_UP, C_HERE, C_DT_RC, C_RC, C_KEEP_PREV, C_P, C_Q, C_RN = range(9)
ST_Q, ST_2, ST_C, ST_3, ST_Z = 0, 6, 8, 9, 11
NSTAGE = 17
B_P1I, B_P1O, B_ER, B_EA, B_P2, B_HI, B_HI2, B_HO = range(8)


def basis_tables():
    j = np.arange(WIDTH + 8, dtype=np.float64)[:, None]
    j[WIDTH:] = -1.0
    m = np.arange(KMAX, dtype=np.float64)[None, :]
    a = 2.0 * np.pi * j * m / NPHI
    base = np.stack([np.cos(a), np.sin(a)])
    turn = 2.0 * np.pi * ((np.arange(16)[:, None] * WIDTH * np.arange(KMAX)[None, :]) % NPHI) / NPHI
    phase = np.stack([np.cos(turn), np.sin(turn)])
    return base.astype(np.float32), phase.astype(np.float32)


def split(x):
    hi = x.astype(BF16)
    lo = (x - hi.astype(F32)).astype(BF16)
    return hi, lo


def dot3(x, b_hi, b_lo, dims):
    hi, lo = split(x)

    def dot(a, b):
        return lax.dot_general(a, b, (dims, ((), ())), preferred_element_type=F32)

    return dot(hi, b_hi) + dot(lo, b_hi) + dot(hi, b_lo)


def kernel(
    er_h, ea_h, eh_h, mr_h, mp_h, mz_h, mat_h, perm_h, cond_h, cut_h, base_h, phase_h,
    ho, o_hz, o_er, o_ea, o_eh, rz1, rz2,
    er, ea, eh, mr, mp, mz, mat,
    perm, cond, cut, base, phase,
    coef, ktab, wts, tab,
    p1s, p1r, p2s, p2r,
    g, rq, s, r2, u, ru, t, v1, v2, ki,
    in_sem, send, recv, bsend, brecv,
):
    phi = lax.axis_index("phi")
    gz = lax.axis_index("gz")
    q = phi % 2
    z = (phi // 2) % 4
    hi_bit = z // 2
    low_bit = z % 2
    gray = (hi_bit + low_bit) % 2
    sib = phi + 1 - 2 * q
    half = (phi // 8) * 8
    dev_z1 = half + (z + 1 - 2 * low_bit) * 2 + q
    dev_z3 = half + (3 - z) * 2 + q
    sib_z1 = dev_z1 + 1 - 2 * q
    sib_z3 = dev_z3 + 1 - 2 * q
    dev_y = (phi + 8) % 16
    nxt = (phi + 1) % 16
    prv = (phi + 15) % 16
    up = (gz + 1) % 8
    down = (gz + 7) % 8
    first_bit = (gray, hi_bit)
    second_bit = (hi_bit, gray)
    first_dev = ((dev_z1, sib_z1), (dev_z3, sib_z3))
    second_dev = (dev_z3, dev_z1)
    pair = tuple(2 * q + b for b in first_bit)

    lane = lax.broadcasted_iota(jnp.int32, (1, 128), 1)

    small = [
        pltpu.make_async_copy(src, dst, in_sem.at[14 + n])
        for n, (src, dst) in enumerate(
            [(base_h, base), (phase_h, phase), (perm_h, perm), (cond_h, cond), (cut_h, cut)]
        )
    ]
    loads = []
    RI = 40
    for n, (src, dst) in enumerate(
        [(eh_h, eh), (er_h, er.at[0:LAYERS]), (ea_h, ea.at[0:LAYERS]), (mr_h, mr), (mp_h, mp), (mz_h, mz), (mat_h, mat)]
    ):
        inner = pltpu.make_async_copy(src.at[:, 0:RI], dst.at[:, 0:RI], in_sem.at[2 * n])
        outer = pltpu.make_async_copy(src.at[:, RI:NR], dst.at[:, RI:NR], in_sem.at[2 * n + 1])
        loads.append((inner, outer))

    barrier = pltpu.get_barrier_semaphore()
    for d in (sib, dev_z1, sib_z1, dev_z3, sib_z3, dev_y, nxt, prv):
        pl.semaphore_signal(barrier, inc=1, device_id={"phi": d}, device_id_type=MESH)
    for d in (up, down):
        pl.semaphore_signal(barrier, inc=1, device_id={"gz": d}, device_id_type=MESH)
    for inner, _ in loads[0:2]:
        inner.start()
    for d in small:
        d.start()
    for inner, _ in loads[2:]:
        inner.start()
    for _, outer in loads:
        outer.start()

    p1s[...] = jnp.zeros_like(p1s)
    p2s[...] = jnp.zeros_like(p2s)

    def pack_first(lo, hi):
        def body(k, _):
            a = pltpu.roll(eh[k, lo:hi], k, 1)
            b = pltpu.roll(er[k, lo:hi], HALO_R + k, 1)
            p1s[lo:hi] = jnp.where(lane == k, a, jnp.where(lane == HALO_R + k, b, p1s[lo:hi]))
            return 0

        lax.fori_loop(0, LAYERS, body, 0)

    loads[0][0].wait()
    loads[1][0].wait()
    pack_first(0, NF)

    pl.semaphore_wait(barrier, 10)

    def border(src, dst, n, dev):
        return pltpu.make_async_remote_copy(
            src_ref=src, dst_ref=dst, send_sem=bsend.at[n], recv_sem=brecv.at[n],
            device_id=dev, device_id_type=MESH,
        )

    b_er = border(er_h.at[0], er.at[LAYERS], B_ER, {"gz": down})
    b_ea = border(ea_h.at[0], ea.at[LAYERS, 0:NR], B_EA, {"gz": down})
    b_p1i = border(p1s.at[0:NF], p1r.at[0:NF], B_P1I, {"phi": prv})
    b_p1o = border(p1s.at[NF:NR], p1r.at[NF:NR], B_P1O, {"phi": prv})
    b_p2 = border(p2s, p2r, B_P2, {"phi": nxt})
    b_hi = border(rz1.at[0, PAIRS, 3:5], rz1.at[0, 0, 3:5], B_HI, {"gz": up})
    b_hi2 = border(rz1.at[1, PAIRS, 3:5], rz1.at[1, 0, 3:5], B_HI2, {"gz": up})
    b_ho = border(ho.at[LAYERS, :, 8:104], ho.at[0, :, 8:104], B_HO, {"gz": up})

    b_p1i.start()
    b_er.start()
    b_ea.start()

    def clear(k, _):
        eh[k, NR : NR + 8] = jnp.zeros((8, 128), F32)
        ea[k, NR : NR + 8] = jnp.zeros((8, 128), F32)
        return 0

    lax.fori_loop(0, LAYERS, clear, 0)
    row = lax.broadcasted_iota(jnp.int32, (NR, 128), 0)
    rn = inner_radius + row.astype(F32)
    rc = rn + 0.5
    inv_rn = 1.0 / rn
    inv_rc = 1.0 / rc
    first = row == 0
    coef[C_DT_RN] = (dt / dphi) * inv_rn
    coef[C_UP] = dt * (rn + 1.0) * inv_rc
    coef[C_HERE] = dt * rn * inv_rc
    coef[C_DT_RC] = (dt / dphi) * inv_rc
    coef[C_RC] = (1.0 / dphi) * inv_rc
    coef[C_KEEP_PREV] = jnp.where(first, 0.0, 1.0)
    coef[C_P] = rc * inv_rn
    coef[C_Q] = jnp.where(first, 0.0, (rc - 1.0) * inv_rn)
    coef[C_RN] = (1.0 / dphi) * inv_rn
    for d in small:
        d.wait()

    for kind in range(2):
        for place, who in enumerate((phi, sib) + first_dev[kind]):
            pc = phase[0, pl.ds(who, 1), :]
            ps = phase[1, pl.ds(who, 1), :]
            if kind == 1 and place < 2:
                tab[:, 1, place * 128 : place * 128 + 128] = tab[:, 0, place * 128 : place * 128 + 128]
            else:
                for part, m in ((0, base[0, 0:128] * pc - base[1, 0:128] * ps), (1, base[1, 0:128] * pc + base[0, 0:128] * ps)):
                    h, l = split(m)
                    tab[0, kind, place * 128 : place * 128 + 128, part * 128 : part * 128 + 128] = h
                    tab[1, kind, place * 128 : place * 128 + 128, part * 128 : part * 128 + 128] = l
            bc, bs = base[0, 128:129], base[1, 128:129]
            lo_row = 512 + place * 32
            for part, m in ((0, bc * pc - bs * ps), (1, bs * pc + bc * ps)):
                h, l = split(jnp.broadcast_to(m, (32, 128)))
                tab[0, kind, lo_row : lo_row + 32, part * 128 : part * 128 + 128] = h
                tab[1, kind, lo_row : lo_row + 32, part * 128 : part * 128 + 128] = l

    for n in range(2, 6):
        loads[n][0].wait()
    b_er.wait_recv()
    b_ea.wait_recv()
    above = jnp.where(gz == 7, 0.0, 1.0)
    er[LAYERS] = er[LAYERS] * above
    ea[LAYERS, 0:NR] = ea[LAYERS, 0:NR] * above
    b_p1i.wait_recv()

    def magnetic(k, lo, hi):
        def ahead(x, n):
            return jnp.where(lane == 127, pltpu.roll(p1r[lo:hi], 127 - n, 1), pltpu.roll(x, 127, 1)) - x

        e_h = eh[k, lo:hi]
        e_r = er[k, lo:hi]
        e_a = ea[k, lo:hi]
        hr = mr[k, lo:hi] - coef[C_DT_RN, lo:hi] * ahead(e_h, k) + dt * (ea[k + 1, lo:hi] - e_a)
        hp = mp[k, lo:hi] - dt * ((er[k + 1, lo:hi] - e_r) - (eh[k, lo + 1 : hi + 1] - e_h))
        hz = (
            mz[k, lo:hi]
            - (coef[C_UP, lo:hi] * ea[k, lo + 1 : hi + 1] - coef[C_HERE, lo:hi] * e_a)
            + coef[C_DT_RC, lo:hi] * ahead(e_r, HALO_R + k)
        )
        return hr, hp, hz

    def factors(k, lo, hi):
        kind = mat[k, lo:hi]
        keep = jnp.broadcast_to(ktab[0, 0, 0:1], kind.shape)
        drive = jnp.broadcast_to(ktab[1, 0, 0:1], kind.shape)
        for number in range(1, NMAT):
            here = kind == number
            keep = jnp.where(here, ktab[0, number, 0:1], keep)
            drive = jnp.where(here, ktab[1, number, 0:1], drive)
        return keep, drive

    def move(f, c, stage, src, dst, dev):
        n = f * CHUNKS + c
        return pltpu.make_async_remote_copy(
            src_ref=src, dst_ref=dst, send_sem=send.at[n, stage], recv_sem=recv.at[n, stage],
            device_id={"phi": dev}, device_id_type=MESH,
        )

    def d_q(f, c):
        out = []
        for a in range(2):
            b = first_bit[a]
            pairs = (2 * q + 1 - b, 2 * (1 - q) + 1 - b, 2 * (1 - q) + b)
            devs = first_dev[a] + (sib,)
            slots = (1, 2, 0)
            for n in range(3):
                src = g.at[f, a, pl.ds(PER_CHUNK * c + 2 * pairs[n], 2)]
                out.append(move(f, c, ST_Q + 3 * a + n, src, rq.at[f, c, a, slots[n]], devs[n]))
        return out

    def d_2(f, c, sets=(0, 1)):
        return [
            move(f, c, ST_2 + a, s.at[f, c, a, 1 - second_bit[a]], r2.at[f, c, a], second_dev[a])
            for a in sets
        ]

    def d_c(f, c):
        return [move(f, c, ST_C, u.at[f, c], ru.at[f, c], dev_y)]

    def d_3(f, c):
        out = []
        for a in range(2):
            own = t.at[f, c, a, second_bit[a]]
            out.append(move(f, c, ST_3 + a, own, own, second_dev[a]))
        return out

    def d_z(f, c, sets=(0, 1)):
        out = []
        for a in sets:
            devs = first_dev[a] + (sib,)
            slots = (1, 2, 0)
            for n in range(3):
                if f == 0:
                    src, dst = v1.at[c, a, slots[n]], rz1.at[a, 1 + 4 * c + pair[a]]
                else:
                    src, dst = v2.at[c, a, slots[n]], rz2.at[a, 4 * c + pair[a]]
                out.append(move(f, c, ST_Z + 3 * a + n, src, dst, devs[n]))
        return out

    def go(copies):
        for d in copies:
            d.start()

    def arrived(copies):
        for d in copies:
            d.wait_recv()

    def stage_1(f, c):
        arrived(d_q(f, c))
        for a in range(2):
            own = g[f, a, pl.ds(PER_CHUNK * c + 2 * pair[a], 2)].reshape(96, 128)
            x = jnp.concatenate([own] + [rq[f, c, a, n].reshape(96, 128) for n in range(3)], axis=1)
            s[f, c, a] = dot3(x, tab[0, a, 0:512], tab[1, a, 0:512], ((1,), (0,))).reshape(2, 3, 16, 256)
            go(d_2(f, c, (a,)))

    def stage_2(f, c):
        arrived(d_2(f, c))
        for a in range(2):
            u[f, c, a] = s[f, c, a, second_bit[a]] + r2[f, c, a]
        go(d_c(f, c))

    def stage_3(f, c):
        arrived(d_c(f, c))
        for a in range(2):
            t[f, c, a, second_bit[a]] = (u[f, c, a] + ru[f, c, a]) * wts[16 * a : 16 * a + 16][None]
        go(d_3(f, c))

    def stage_4(f, c):
        arrived(d_3(f, c))
        for a in range(2):
            x = t[f, c, a].reshape(96, 256)
            if f == 0:
                y = dot3(x, tab[0, a], tab[1, a], ((1,), (1,))).reshape(6, 16, 640)
                border_lanes = lane % 32
                before = y[0, :, 512:640]
                for n, source in ((1, 2), (2, 3), (3, 5)):
                    before = jnp.where(border_lanes == n, y[source, :, 512:640], before)
                for n in range(3):
                    v1[c, a, n, 0:6] = y[:, :, 128 * n + 128 : 128 * n + 256]
                    v1[c, a, n, 6] = before
                go(d_z(f, c, (a,)))
                rz1[a, 1 + 4 * c + pair[a], 0:6] = y[:, :, 0:128]
                rz1[a, 1 + 4 * c + pair[a], 6] = before
            else:
                y = dot3(x, tab[0, a, 0:512], tab[1, a, 0:512], ((1,), (1,))).reshape(6, 16, 512)
                for n in range(3):
                    v2[c, a, n] = y[:, :, 128 * n + 128 : 128 * n + 256]
                go(d_z(f, c, (a,)))
                rz2[a, 4 * c + pair[a]] = y[:, :, 0:128]

    def put(f, k, n, x):
        g[f, 0, k, n] = x[0:16]
        g[f, 1, k, n] = x[16:32]

    def begin_h(c):
        def body(k, _):
            for n, x in enumerate(magnetic(k, 0, NF)):
                put(0, k, n, x)
            return 0

        lax.fori_loop(PER_CHUNK * c, PER_CHUNK * c + PER_CHUNK, body, 0)
        go(d_q(0, c))

    below = jnp.where(gz == 0, 0.0, 1.0)

    def electric_inner(k, _):
        at, l = 1 + k // 2, k % 2
        prev_at, prev_l = (k + 1) // 2, (k + 1) % 2
        owner = at - 1 - 4 * (k // 8)

        def get(place, which, n):
            return jnp.concatenate([rz1[0, place, 3 * which + n], rz1[1, place, 3 * which + n]], axis=0)

        hr, hp, hz = (get(at, l, n) for n in range(3))
        hr_below, hp_below = get(prev_at, prev_l, 0), get(prev_at, prev_l, 1)
        own_q, own_b = owner // 2, owner % 2
        off_q = own_q + q - 2 * own_q * q
        marks = []
        for a in range(2):
            off_b = own_b + first_bit[a] - 2 * own_b * first_bit[a]
            marks.append(32 * (off_q + 2 * off_b) + 2 * l)

        def behind(x, n):
            edge = jnp.concatenate(
                [pltpu.roll(rz1[a, at, 6], (128 - marks[a] - n) % 128, 1) for a in range(2)], axis=0
            )
            return x - jnp.where(lane == 0, edge, pltpu.roll(x, 1, 1))

        keep, drive = ki[k, 0], ki[k, 1]
        back = pltpu.roll(hp, 1, 0)
        put(1, k, 0, keep * er[k, 0:NF] + drive * (coef[C_RC, 0:NF] * behind(hz, 1) - (hp - hp_below)))
        put(
            1, k, 1,
            keep * ea[k, 0:NF] + drive * ((hr - hr_below) - (hp - coef[C_KEEP_PREV, 0:NF] * back)),
        )
        put(
            1, k, 2,
            keep * eh[k, 0:NF]
            + drive * (coef[C_P, 0:NF] * hp - coef[C_Q, 0:NF] * back - coef[C_RN, 0:NF] * behind(hr, 0)),
        )
        return 0

    def begin_e(c):
        lax.fori_loop(PER_CHUNK * c, PER_CHUNK * c + PER_CHUNK, electric_inner, 0)
        go(d_q(1, c))

    def inner_factors(k, _):
        keep, drive = factors(k, 0, NF)
        ki[k, 0] = keep
        ki[k, 1] = drive
        return 0

    def tables():
        for number in range(NMAT):
            eps = jnp.full((8, 128), perm[number], F32)
            sig = jnp.full((8, 128), cond[number], F32)
            loss = sig * dt / (2.0 * eps)
            ktab[0, number] = (1.0 - loss) / (1.0 + loss)
            ktab[1, number] = dt / (eps * (1.0 + loss))
        mode = lax.broadcasted_iota(jnp.int32, (NF, 128), 1)
        wrow = lax.broadcasted_iota(jnp.int32, (NF, 128), 0)
        cuts = jnp.zeros((NF, 128), jnp.int32)
        for number in range(NF):
            cuts = jnp.where(wrow == number, cut[number], cuts)
        weight = jnp.where(mode == 0, 1.0 / NPHI, 2.0 / NPHI)
        weight = jnp.where(mode <= cuts, weight, 0.0)
        wts[:, 0:128] = weight
        wts[:, 128:256] = weight

    def outer_h(k, _):
        hr, hp, hz = magnetic(k, NF, NR)
        ho[k + 1, 0, 8:104] = hr
        ho[k + 1, 1, 8:104] = hp
        o_hz[k] = hz
        p2s[...] = jnp.where(
            lane == k,
            pltpu.roll(hr, k + 1, 1),
            jnp.where(lane == HALO_R + k, pltpu.roll(hz, HALO_R + k + 1, 1), p2s[...]),
        )
        return 0

    def last_inner_row(k, _):
        ho[k + 1, 1, 0:8] = rz1[1, 1 + k // 2, 3 * (k % 2) + 1, 8:16]
        return 0

    def outer_e(k, _):
        hr, hp, hz = ho[k + 1, 0, 8:104], ho[k + 1, 1, 8:104], o_hz[k]
        back = ho[k + 1, 1, 7:103]
        keep, drive = factors(k, NF, NR)

        def behind(x, n):
            return x - jnp.where(lane == 0, pltpu.roll(p2r[...], (128 - n) % 128, 1), pltpu.roll(x, 1, 1))

        o_er[k] = keep * er[k, NF:NR] + drive * (coef[C_RC, NF:NR] * behind(hz, HALO_R + k) - (hp - ho[k, 1, 8:104]))
        o_ea[k] = keep * ea[k, NF:NR] + drive * ((hr - ho[k, 0, 8:104]) - (hp - back))
        o_eh[k] = keep * eh[k, NF:NR] + drive * (
            coef[C_P, NF:NR] * hp - coef[C_Q, NF:NR] * back - coef[C_RN, NF:NR] * behind(hr, k)
        )
        return 0

    def run(body, lo, hi):
        lax.fori_loop(lo, hi, body, 0)

    begin_h(0)
    begin_h(1)
    begin_h(2)
    tables()
    loads[6][0].wait()
    stage_1(0, 0)
    for n in range(7):
        loads[n][1].wait()
    pack_first(NF, NR)
    b_p1o.start()
    stage_1(0, 1)
    run(inner_factors, 0, 12)
    stage_2(0, 0)
    stage_1(0, 2)
    run(inner_factors, 12, 24)
    stage_2(0, 1)
    b_p1o.wait_recv()
    run(outer_h, 18, 24)
    stage_3(0, 0)
    stage_2(0, 2)
    b_ho.start()
    run(outer_h, 12, 18)
    stage_3(0, 1)
    stage_4(0, 0)
    run(outer_h, 6, 12)
    stage_3(0, 2)
    stage_4(0, 1)
    run(outer_h, 0, 6)
    b_p2.start()
    arrived(d_z(0, 0))
    stage_4(0, 2)
    arrived(d_z(0, 1))
    begin_e(1)
    arrived(d_z(0, 2))
    b_hi.start()
    b_hi2.start()
    begin_e(2)
    b_hi.wait_recv()
    b_hi2.wait_recv()
    for a in range(2):
        rz1[a, 0, 3:5] = rz1[a, 0, 3:5] * below
    begin_e(0)
    stage_1(1, 1)
    run(last_inner_row, 0, LAYERS)
    b_p2.wait_recv()
    b_ho.wait_recv()
    ho[0, :, 8:104] = ho[0, :, 8:104] * below
    stage_1(1, 2)
    run(outer_e, 0, 4)
    stage_2(1, 1)
    stage_1(1, 0)
    run(outer_e, 4, 8)
    stage_2(1, 2)
    run(outer_e, 8, 12)
    stage_3(1, 1)
    stage_2(1, 0)
    run(outer_e, 12, 16)
    stage_3(1, 2)
    stage_4(1, 1)
    run(outer_e, 16, 20)
    stage_3(1, 0)
    stage_4(1, 2)
    run(outer_e, 20, 24)
    stage_4(1, 0)
    for c in (1, 2, 0):
        arrived(d_z(1, c))

    for f in range(2):
        for c in range(CHUNKS):
            for kind in (d_q, d_2, d_c, d_3, d_z):
                for d in kind(f, c):
                    d.wait_send()
    for d in (b_er, b_ea, b_p1i, b_p1o, b_p2, b_hi, b_hi2, b_ho):
        d.wait_send()


def local(er, ea, eh, mr, mp, mz, material, permittivity, conductivity, mode_cutoff):
    base, phase = basis_tables()
    anywhere = pl.BlockSpec(memory_space=pltpu.HBM)
    vmem = pl.BlockSpec(memory_space=pltpu.VMEM)

    def scratch(*shape, dtype=F32):
        return pltpu.VMEM(shape, dtype)

    field = (LAYERS, NR, WIDTH)
    outer = (LAYERS, OUT, WIDTH)
    held = (
        scratch(LAYERS + 1, 2, OUT + 8, WIDTH),
        scratch(*outer),
        scratch(*outer),
        scratch(*outer),
        scratch(*outer),
        scratch(2, PAIRS + 1, 7, 16, WIDTH),
        scratch(2, PAIRS, 6, 16, WIDTH),
    )
    step = pl.pallas_call(
        kernel,
        out_shape=held,
        in_specs=[anywhere] * 12,
        out_specs=tuple([vmem] * 7),
        scratch_shapes=[
            scratch(LAYERS + 1, NR, WIDTH),
            scratch(LAYERS + 1, NR + 8, WIDTH),
            scratch(LAYERS, NR + 8, WIDTH),
            scratch(*field),
            scratch(*field),
            scratch(*field),
            scratch(*field, dtype=jnp.int32),
            pltpu.SMEM((NMAT,), F32),
            pltpu.SMEM((NMAT,), F32),
            pltpu.SMEM((NF,), jnp.int32),
            scratch(*base.shape),
            scratch(*phase.shape),
            scratch(9, NR, 128),
            scratch(2, NMAT, 8, 128),
            scratch(NF, 256),
            scratch(2, 2, 640, 256, dtype=BF16),
            scratch(NR, 128),
            scratch(NR, 128),
            scratch(OUT, 128),
            scratch(OUT, 128),
            scratch(2, 2, LAYERS, 3, 16, 128),
            scratch(2, CHUNKS, 2, 3, 2, 3, 16, 128),
            scratch(2, CHUNKS, 2, 2, 3, 16, 256),
            scratch(2, CHUNKS, 2, 3, 16, 256),
            scratch(2, CHUNKS, 2, 3, 16, 256),
            scratch(2, CHUNKS, 2, 3, 16, 256),
            scratch(2, CHUNKS, 2, 2, 3, 16, 256),
            scratch(CHUNKS, 2, 3, 7, 16, 128),
            scratch(CHUNKS, 2, 3, 6, 16, 128),
            scratch(LAYERS, 2, NF, 128),
            pltpu.SemaphoreType.DMA((19,)),
            pltpu.SemaphoreType.DMA((2 * CHUNKS, NSTAGE)),
            pltpu.SemaphoreType.DMA((2 * CHUNKS, NSTAGE)),
            pltpu.SemaphoreType.DMA((8,)),
            pltpu.SemaphoreType.DMA((8,)),
        ],
        compiler_params=pltpu.CompilerParams(
            collective_id=0, has_side_effects=True, vmem_limit_bytes=40 * 1024 * 1024
        ),
        name="yee_step",
    )
    operands = (
        er, ea, eh, mr, mp, mz, material, permittivity, conductivity, mode_cutoff,
        jnp.asarray(base), jnp.asarray(phase),
    )
    return rows_out(*step(*(pltpu.with_memory_space_constraint(x, pltpu.HBM) for x in operands)))


def rows_out(ho, o_hz, o_er, o_ea, o_eh, rz1, rz2):
    vmem = pl.BlockSpec(memory_space=pltpu.VMEM)
    hbm = pl.BlockSpec(memory_space=pltpu.HBM)
    return pl.pallas_call(
        write_kernel,
        out_shape=tuple(jax.ShapeDtypeStruct((LAYERS, NR, WIDTH), F32) for _ in range(6)),
        in_specs=[vmem] * 7,
        out_specs=tuple([hbm] * 6),
        scratch_shapes=[pltpu.SemaphoreType.DMA((40,))],
        compiler_params=pltpu.CompilerParams(vmem_limit_bytes=1024 * 1024),
        name="write_fields",
    )(ho, o_hz, o_er, o_ea, o_eh, rz1, rz2)

def write_kernel(ho, o_hz, o_er, o_ea, o_eh, rz1, rz2, w_er, w_ea, w_eh, w_hr, w_hp, w_hz, sem):
    copies = []

    def add(src, dst):
        copies.append(pltpu.make_async_copy(src, dst, sem.at[len(copies)]))

    for o, w in ((o_hz, w_hz), (o_er, w_er), (o_ea, w_ea), (o_eh, w_eh)):
        add(o, w.at[:, NF:NR])
    for n, w in ((0, w_hr), (1, w_hp)):
        add(ho.at[1 : LAYERS + 1, n, 8:104], w.at[:, NF:NR])
    for l in range(2):
        for a in range(2):
            rows = slice(16 * a, 16 * a + 16)
            for n, w in enumerate((w_hr, w_hp, w_hz)):
                add(rz1.at[a, 1 : PAIRS + 1, 3 * l + n], w.reshape(PAIRS, 2, NR, WIDTH).at[:, l, rows])
            for n, w in enumerate((w_er, w_ea, w_eh)):
                add(rz2.at[a, :, 3 * l + n], w.reshape(PAIRS, 2, NR, WIDTH).at[:, l, rows])
    for d in copies:
        d.start()
    for d in copies:
        d.wait()


def solution(mesh):
    field = P("gz", None, "phi")
    return jax.shard_map(
        local,
        mesh=mesh,
        in_specs=(field,) * 7 + (P(),) * 3,
        out_specs=(field,) * 6,
        check_vma=False,
    )
```

```python
import math

import jax
import jax.numpy as jnp
import numpy as np
from jax import lax
from jax.experimental import pallas as pl
from jax.experimental.pallas import tpu as pltpu
from jax.sharding import PartitionSpec as P

KMAX = 128
NF = 32
NMAT = 8
NPHI = 2048
NR = 128
OUT = NR - NF
LAYERS = 24
WIDTH = 128
CHUNKS = 3
PER_CHUNK = LAYERS // CHUNKS
HELD = PER_CHUNK // 4
HALO_R = 32

inner_radius = 64.0
dt = 0.2
dphi = 2.0 * math.pi / NPHI
MESH = pl.DeviceIdType.MESH
F32 = jnp.float32
BF16 = jnp.bfloat16

C_DT_RN, C_UP, C_HERE, C_DT_RC, C_RC, C_KEEP_PREV, C_P, C_Q, C_RN = range(9)
ST_Q, ST_2, ST_C, ST_3, ST_Z = 0, 6, 8, 9, 11
NSTAGE = 17
B_P1O, B_ER, B_EA, B_P2, B_HO, B_P1Q, B_HI = 0, 1, 2, 3, 4, 5, 10
NBORDER = 20


def basis_tables():
    j = np.arange(WIDTH + 8, dtype=np.float64)[:, None]
    j[WIDTH:] = -1.0
    m = np.arange(KMAX, dtype=np.float64)[None, :]
    a = 2.0 * np.pi * j * m / NPHI
    base = np.stack([np.cos(a), np.sin(a)])
    turn = 2.0 * np.pi * ((np.arange(16)[:, None] * WIDTH * np.arange(KMAX)[None, :]) % NPHI) / NPHI
    phase = np.stack([np.cos(turn), np.sin(turn)])
    return base.astype(np.float32), phase.astype(np.float32)


def split(x):
    hi = x.astype(BF16)
    lo = (x - hi.astype(F32)).astype(BF16)
    return hi, lo


def dot3(x, b_hi, b_lo, dims):
    hi, lo = split(x)

    def dot(a, b):
        return lax.dot_general(a, b, (dims, ((), ())), preferred_element_type=F32)

    m = x.shape[0]
    high = dot(jnp.concatenate([hi, lo], axis=0), b_hi)
    return high[0:m] + high[m : 2 * m] + dot(hi, b_lo)


def kernel(
    er_h, ea_h, eh_h, mr_h, mp_h, mz_h, mat_h, perm_h, cond_h, cut_h, base_h, phase_h,
    ho, o_hz, o_er, o_ea, o_eh, rz1, rz2,
    er, ea, eh, mr, mp, mz, mat,
    perm, cond, cut, base, phase,
    coef, ktab, wts, tab,
    p1s, p1r, p1q, p2s, p2r,
    g, rq, s, r2, u, ru, t, v1, v2, ki,
    in_sem, send, recv, bsend, brecv,
):
    phi = lax.axis_index("phi")
    gz = lax.axis_index("gz")
    q = phi % 2
    z = (phi // 2) % 4
    hi_bit = z // 2
    low_bit = z % 2
    gray = (hi_bit + low_bit) % 2
    sib = phi + 1 - 2 * q
    half = (phi // 8) * 8
    dev_z1 = half + (z + 1 - 2 * low_bit) * 2 + q
    dev_z3 = half + (3 - z) * 2 + q
    sib_z1 = dev_z1 + 1 - 2 * q
    sib_z3 = dev_z3 + 1 - 2 * q
    dev_y = (phi + 8) % 16
    nxt = (phi + 1) % 16
    prv = (phi + 15) % 16
    up = (gz + 1) % 8
    down = (gz + 7) % 8
    first_bit = (gray, hi_bit)
    second_bit = (hi_bit, gray)
    first_dev = ((dev_z1, sib_z1), (dev_z3, sib_z3))
    second_dev = (dev_z3, dev_z1)
    pair = tuple(2 * q + b for b in first_bit)

    lane = lax.broadcasted_iota(jnp.int32, (1, 128), 1)

    small = [
        pltpu.make_async_copy(src, dst, in_sem.at[14 + n])
        for n, (src, dst) in enumerate(
            [(base_h, base), (phase_h, phase), (perm_h, perm), (cond_h, cond), (cut_h, cut)]
        )
    ]
    loads = []
    RI = 40
    for n, (src, dst) in enumerate(
        [(eh_h, eh), (er_h, er.at[0:LAYERS]), (ea_h, ea.at[0:LAYERS]), (mr_h, mr), (mp_h, mp), (mz_h, mz), (mat_h, mat)]
    ):
        inner = pltpu.make_async_copy(src.at[:, 0:RI], dst.at[:, 0:RI], in_sem.at[2 * n])
        outer = pltpu.make_async_copy(src.at[:, RI:NR], dst.at[:, RI:NR], in_sem.at[2 * n + 1])
        loads.append((inner, outer))

    barrier = pltpu.get_barrier_semaphore()
    quads = (sib, dev_z1, sib_z1, dev_z3, sib_z3)
    for d in quads + (dev_y, nxt, prv):
        pl.semaphore_signal(barrier, inc=1, device_id={"phi": d}, device_id_type=MESH)
    for slab in (up, down):
        for d in quads + (phi,):
            pl.semaphore_signal(barrier, inc=1, device_id={"phi": d, "gz": slab}, device_id_type=MESH)
    for inner, _ in loads[0:2]:
        inner.start()
    for d in small:
        d.start()
    for inner, _ in loads[2:]:
        inner.start()
    for _, outer in loads:
        outer.start()

    p1s[...] = jnp.zeros_like(p1s)
    p2s[...] = jnp.zeros_like(p2s)

    def pack_first(lo, hi):
        def body(k, _):
            a = pltpu.roll(eh[k, lo:hi], k, 1)
            b = pltpu.roll(er[k, lo:hi], HALO_R + k, 1)
            p1s[lo:hi] = jnp.where(lane == k, a, jnp.where(lane == HALO_R + k, b, p1s[lo:hi]))
            return 0

        lax.fori_loop(0, LAYERS, body, 0)

    def clear(k, _):
        eh[k, NR : NR + 8] = jnp.zeros((8, 128), F32)
        ea[k, NR : NR + 8] = jnp.zeros((8, 128), F32)
        return 0

    lax.fori_loop(0, LAYERS, clear, 0)
    row = lax.broadcasted_iota(jnp.int32, (NR, 128), 0)
    rn = inner_radius + row.astype(F32)
    rc = rn + 0.5
    inv_rn = 1.0 / rn
    inv_rc = 1.0 / rc
    first = row == 0
    coef[C_DT_RN] = (dt / dphi) * inv_rn
    coef[C_UP] = dt * (rn + 1.0) * inv_rc
    coef[C_HERE] = dt * rn * inv_rc
    coef[C_DT_RC] = (dt / dphi) * inv_rc
    coef[C_RC] = (1.0 / dphi) * inv_rc
    coef[C_KEEP_PREV] = jnp.where(first, 0.0, 1.0)
    coef[C_P] = rc * inv_rn
    coef[C_Q] = jnp.where(first, 0.0, (rc - 1.0) * inv_rn)
    coef[C_RN] = (1.0 / dphi) * inv_rn
    def border(src, dst, n, dev, arrival=None):
        return pltpu.make_async_remote_copy(
            src_ref=src, dst_ref=dst, send_sem=bsend.at[n], recv_sem=brecv.at[n if arrival is None else arrival],
            device_id=dev, device_id_type=MESH,
        )

    b_er = border(er_h.at[0], er.at[LAYERS], B_ER, {"gz": down})
    b_ea = border(ea_h.at[0], ea.at[LAYERS, 0:NR], B_EA, {"gz": down})
    b_p1q = [border(p1s.at[0:NF], p1q.at[n], B_P1Q + n, {"phi": d}) for n, d in enumerate(quads)]
    b_p1o = border(p1s.at[NF:NR], p1r, B_P1O, {"phi": prv})
    b_p2 = border(p2s, p2r, B_P2, {"phi": nxt})
    b_ho = border(ho.at[LAYERS, :, 8:104], ho.at[0, :, 8:104], B_HO, {"gz": up})

    def magnetic(k, lo, hi):
        def ahead(x, n):
            edge = 0.0 if lo == 0 else pltpu.roll(p1r[...], 127 - n, 1)
            return jnp.where(lane == 127, edge, pltpu.roll(x, 127, 1)) - x

        e_h = eh[k, lo:hi]
        e_r = er[k, lo:hi]
        e_a = ea[k, lo:hi]
        hr = mr[k, lo:hi] - coef[C_DT_RN, lo:hi] * ahead(e_h, k) + dt * (ea[k + 1, lo:hi] - e_a)
        hp = mp[k, lo:hi] - dt * ((er[k + 1, lo:hi] - e_r) - (eh[k, lo + 1 : hi + 1] - e_h))
        hz = (
            mz[k, lo:hi]
            - (coef[C_UP, lo:hi] * ea[k, lo + 1 : hi + 1] - coef[C_HERE, lo:hi] * e_a)
            + coef[C_DT_RC, lo:hi] * ahead(e_r, HALO_R + k)
        )
        return hr, hp, hz

    def factors(k, lo, hi):
        kind = mat[k, lo:hi]
        keep = jnp.broadcast_to(ktab[0, 0, 0:1], kind.shape)
        drive = jnp.broadcast_to(ktab[1, 0, 0:1], kind.shape)
        for number in range(1, NMAT):
            here = kind == number
            keep = jnp.where(here, ktab[0, number, 0:1], keep)
            drive = jnp.where(here, ktab[1, number, 0:1], drive)
        return keep, drive

    def move(f, c, stage, src, dst, dev):
        n = f * CHUNKS + c
        return pltpu.make_async_remote_copy(
            src_ref=src, dst_ref=dst, send_sem=send.at[n, stage], recv_sem=recv.at[n, stage],
            device_id={"phi": dev}, device_id_type=MESH,
        )

    def d_q(f, c):
        out = []
        for a in range(2):
            b = first_bit[a]
            owners = (2 * q + 1 - b, 2 * (1 - q) + 1 - b, 2 * (1 - q) + b)
            devs = first_dev[a] + (sib,)
            slots = (1, 2, 0)
            for n in range(3):
                src = g.at[f, a, pl.ds(PER_CHUNK * c + HELD * owners[n], HELD)]
                out.append(move(f, c, ST_Q + 3 * a + n, src, rq.at[f, c, a, slots[n]], devs[n]))
        return out

    def eight(bit):
        return pl.ds(pl.multiple_of(8 * bit, 8), 8)

    def d_2(f, c, sets=(0, 1)):
        return [
            move(f, c, ST_2 + a, s.at[f, c, a, :, :, eight(1 - second_bit[a])], r2.at[f, c, a], second_dev[a])
            for a in sets
        ]

    def d_c(f, c):
        return [move(f, c, ST_C, u.at[f, c], ru.at[f, c], dev_y)]

    def d_3(f, c):
        out = []
        for a in range(2):
            own = t.at[f, c, a, :, :, eight(second_bit[a])]
            out.append(move(f, c, ST_3 + a, own, own, second_dev[a]))
        return out

    def d_z(f, c, sets=(0, 1)):
        out = []
        for a in sets:
            devs = first_dev[a] + (sib,)
            slots = (1, 2, 0)
            for n in range(3):
                if f == 0:
                    src, dst = v1.at[c, a, slots[n]], rz1.at[a, pl.ds(1 + PER_CHUNK * c + HELD * pair[a], HELD)]
                else:
                    src, dst = v2.at[c, a, slots[n]], rz2.at[a, pl.ds(PER_CHUNK * c + HELD * pair[a], HELD)]
                out.append(move(f, c, ST_Z + 3 * a + n, src, dst, devs[n]))
        return out

    def d_up(a):
        devs = (sib,) + first_dev[a] + (phi,)
        srcs = [v1.at[CHUNKS - 1, a, n, HELD - 1, 0:2] for n in range(3)] + [rz1.at[a, LAYERS, 0:2]]
        return [
            border(srcs[n], rz1.at[a, 0, 0:2], B_HI + 4 * a + n, {"phi": devs[n], "gz": up}, B_HI + a)
            for n in range(4)
        ]

    started = []

    def go(copies):
        for d in copies:
            d.start()
            started.append(d)

    def arrived(copies):
        for d in copies:
            d.wait_recv()

    def stage_1(f, c):
        arrived(d_q(f, c))
        for a in range(2):
            k = PER_CHUNK * c + HELD * pair[a]
            own = g[f, a, pl.ds(k, HELD)].reshape(48 * HELD, 128)
            parts = [own] + [rq[f, c, a, n].reshape(48 * HELD, 128) for n in range(3)]
            width = 512
            if f == 0:
                rows = slice(16 * a, 16 * a + 16)
                tiles = [p1s[rows]] + [p1q[n, rows] for n in ((0, 1, 2), (0, 3, 4))[a]]
                extra = []
                for l in range(HELD):
                    height = jnp.zeros((16, 128), F32)
                    radial = jnp.zeros((16, 128), F32)
                    for m in range(4):
                        here = lane == 32 * m
                        height = jnp.where(here, pltpu.roll(tiles[m], (32 * m + 128 - k - l) % 128, 1), height)
                        radial = jnp.where(here, pltpu.roll(tiles[m], (32 * m + 128 - HALO_R - k - l) % 128, 1), radial)
                    extra += [-coef[C_DT_RN, rows] * height, jnp.zeros((16, 128), F32), coef[C_DT_RC, rows] * radial]
                parts.append(jnp.concatenate(extra, axis=0))
                width = 640
            x = jnp.concatenate(parts, axis=1)
            s[f, c, a] = dot3(x, tab[0, a, 0:width], tab[1, a, 0:width], ((1,), (0,))).reshape(HELD, 3, 16, 256)
            go(d_2(f, c, (a,)))

    def stage_2(f, c):
        arrived(d_2(f, c))
        for a in range(2):
            u[f, c, a] = s[f, c, a, :, :, eight(second_bit[a])] + r2[f, c, a]
        go(d_c(f, c))

    def stage_3(f, c):
        arrived(d_c(f, c))
        for a in range(2):
            w = wts[pl.ds(pl.multiple_of(16 * a + 8 * second_bit[a], 8), 8)]
            t[f, c, a, :, :, eight(second_bit[a])] = (u[f, c, a] + ru[f, c, a]) * w[None, None]
        go(d_3(f, c))

    def stage_4(f, c):
        arrived(d_3(f, c))
        for a in range(2):
            x = t[f, c, a].reshape(48 * HELD, 256)
            k = PER_CHUNK * c + HELD * pair[a]
            if f == 0:
                y = dot3(x, tab[0, a], tab[1, a], ((1,), (1,))).reshape(HELD, 3, 16, 640)
                before = jnp.where(lane % 32 == 0, y[:, 0, :, 512:640], y[:, 2, :, 512:640])
                for n in range(3):
                    v1[c, a, n, :, 0:3] = y[..., 128 * n + 128 : 128 * n + 256]
                    v1[c, a, n, :, 3] = before
                go(d_z(f, c, (a,)))
                rz1[a, pl.ds(1 + k, HELD), 0:3] = y[..., 0:128]
                rz1[a, pl.ds(1 + k, HELD), 3] = before
                if c == CHUNKS - 1:

                    @pl.when(pair[a] == 3)
                    def _():
                        for d in d_up(a):
                            d.start()

            else:
                y = dot3(x, tab[0, a, 0:512], tab[1, a, 0:512], ((1,), (1,))).reshape(HELD, 3, 16, 512)
                for n in range(3):
                    v2[c, a, n] = y[..., 128 * n + 128 : 128 * n + 256]
                go(d_z(f, c, (a,)))
                rz2[a, pl.ds(k, HELD)] = y[..., 0:128]

    def stage_5(f, c):
        arrived(d_z(f, c))

    def put(f, k, n, x):
        g[f, 0, k, n] = x[0:16]
        g[f, 1, k, n] = x[16:32]

    def update_h(lo, hi):
        def body(k, _):
            for n, x in enumerate(magnetic(k, 0, NF)):
                put(0, k, n, x)
            return 0

        lax.fori_loop(lo, hi, body, 0)

    below = jnp.where(gz == 0, 0.0, 1.0)

    def electric_inner(k, _):
        owner = (k % PER_CHUNK) // HELD

        def get(place, n):
            return jnp.concatenate([rz1[0, place, n], rz1[1, place, n]], axis=0)

        hr, hp, hz = (get(k + 1, n) for n in range(3))
        hr_below, hp_below = get(k, 0), get(k, 1)
        own_q, own_b = owner // 2, owner % 2
        off_q = own_q + q - 2 * own_q * q
        marks = []
        for a in range(2):
            off_b = own_b + first_bit[a] - 2 * own_b * first_bit[a]
            marks.append(32 * (off_q + 2 * off_b))

        def behind(x, n):
            edge = jnp.concatenate(
                [pltpu.roll(rz1[a, k + 1, 3], (128 - marks[a] - n) % 128, 1) for a in range(2)], axis=0
            )
            return x - jnp.where(lane == 0, edge, pltpu.roll(x, 1, 1))

        keep, drive = ki[k, 0], ki[k, 1]
        back = pltpu.roll(hp, 1, 0)
        put(1, k, 0, keep * er[k, 0:NF] + drive * (coef[C_RC, 0:NF] * behind(hz, 1) - (hp - hp_below)))
        put(
            1, k, 1,
            keep * ea[k, 0:NF] + drive * ((hr - hr_below) - (hp - coef[C_KEEP_PREV, 0:NF] * back)),
        )
        put(
            1, k, 2,
            keep * eh[k, 0:NF]
            + drive * (coef[C_P, 0:NF] * hp - coef[C_Q, 0:NF] * back - coef[C_RN, 0:NF] * behind(hr, 0)),
        )
        return 0

    def begin_e(c):
        lax.fori_loop(PER_CHUNK * c, PER_CHUNK * c + PER_CHUNK, electric_inner, 0)
        go(d_q(1, c))

    def inner_factors(k, _):
        keep, drive = factors(k, 0, NF)
        ki[k, 0] = keep
        ki[k, 1] = drive
        return 0

    def basis():
        for d in small:
            d.wait()

        for kind in range(2):
            for place, who in enumerate((phi, sib) + first_dev[kind]):
                pc = phase[0, pl.ds(who, 1), :]
                ps = phase[1, pl.ds(who, 1), :]
                if kind == 1 and place < 2:
                    tab[:, 1, place * 128 : place * 128 + 128] = tab[:, 0, place * 128 : place * 128 + 128]
                else:
                    for part, m in ((0, base[0, 0:128] * pc - base[1, 0:128] * ps), (1, base[1, 0:128] * pc + base[0, 0:128] * ps)):
                        h, l = split(m)
                        tab[0, kind, place * 128 : place * 128 + 128, part * 128 : part * 128 + 128] = h
                        tab[1, kind, place * 128 : place * 128 + 128, part * 128 : part * 128 + 128] = l
                bc, bs = base[0, 128:129], base[1, 128:129]
                lo_row = 512 + place * 32
                for part, m in ((0, bc * pc - bs * ps), (1, bs * pc + bc * ps)):
                    h, l = split(jnp.broadcast_to(m, (32, 128)))
                    tab[0, kind, lo_row : lo_row + 32, part * 128 : part * 128 + 128] = h
                    tab[1, kind, lo_row : lo_row + 32, part * 128 : part * 128 + 128] = l


    def tables():
        for number in range(NMAT):
            eps = jnp.full((8, 128), perm[number], F32)
            sig = jnp.full((8, 128), cond[number], F32)
            loss = sig * dt / (2.0 * eps)
            ktab[0, number] = (1.0 - loss) / (1.0 + loss)
            ktab[1, number] = dt / (eps * (1.0 + loss))
        mode = lax.broadcasted_iota(jnp.int32, (NF, 128), 1)
        wrow = lax.broadcasted_iota(jnp.int32, (NF, 128), 0)
        cuts = jnp.zeros((NF, 128), jnp.int32)
        for number in range(NF):
            cuts = jnp.where(wrow == number, cut[number], cuts)
        weight = jnp.where(mode == 0, 1.0 / NPHI, 2.0 / NPHI)
        weight = jnp.where(mode <= cuts, weight, 0.0)
        wts[:, 0:128] = weight
        wts[:, 128:256] = weight

    def outer_h(k, _):
        hr, hp, hz = magnetic(k, NF, NR)
        ho[k + 1, 0, 8:104] = hr
        ho[k + 1, 1, 8:104] = hp
        o_hz[k] = hz
        p2s[...] = jnp.where(
            lane == k,
            pltpu.roll(hr, k + 1, 1),
            jnp.where(lane == HALO_R + k, pltpu.roll(hz, HALO_R + k + 1, 1), p2s[...]),
        )
        return 0

    def last_inner_row(k, _):
        ho[k + 1, 1, 0:8] = rz1[1, k + 1, 1, 8:16]
        return 0

    def outer_e(k, _):
        hr, hp, hz = ho[k + 1, 0, 8:104], ho[k + 1, 1, 8:104], o_hz[k]
        back = ho[k + 1, 1, 7:103]
        keep, drive = factors(k, NF, NR)

        def behind(x, n):
            return x - jnp.where(lane == 0, pltpu.roll(p2r[...], (128 - n) % 128, 1), pltpu.roll(x, 1, 1))

        o_er[k] = keep * er[k, NF:NR] + drive * (coef[C_RC, NF:NR] * behind(hz, HALO_R + k) - (hp - ho[k, 1, 8:104]))
        o_ea[k] = keep * ea[k, NF:NR] + drive * ((hr - ho[k, 0, 8:104]) - (hp - back))
        o_eh[k] = keep * eh[k, NF:NR] + drive * (
            coef[C_P, NF:NR] * hp - coef[C_Q, NF:NR] * back - coef[C_RN, NF:NR] * behind(hr, k)
        )
        return 0

    def run(body, lo, hi):
        lax.fori_loop(lo, hi, body, 0)

    def outer_loaded():
        for n in range(7):
            loads[n][1].wait()
        pack_first(NF, NR)
        go([b_p1o])

    def layer_above():
        arrived([b_er, b_ea])
        above = jnp.where(gz == 7, 0.0, 1.0)
        er[LAYERS] = er[LAYERS] * above
        ea[LAYERS, 0:NR] = ea[LAYERS, 0:NR] * above

    def begin_h(c):
        update_h(PER_CHUNK * c, PER_CHUNK * c + PER_CHUNK)
        go(d_q(0, c))

    def layer_below():
        for a in range(2):
            arrived(d_up(a)[0:1])
            rz1[a, 0, 0:2] = rz1[a, 0, 0:2] * below

    def outer_borders():
        arrived([b_p2, b_ho])
        ho[0, :, 8:104] = ho[0, :, 8:104] * below

    def drain():
        while started:
            started.pop().wait_send()

    for n in range(6):
        loads[n][0].wait()
    pack_first(0, NF)
    update_h(0, PER_CHUNK)
    pl.semaphore_wait(barrier, 20)
    go([b_er, b_ea] + d_q(0, 0) + b_p1q)
    if CHUNKS > 2:
        begin_h(1)
    basis()
    layer_above()
    if CHUNKS == 2:
        begin_h(1)
    tables()
    loads[6][0].wait()
    arrived(b_p1q)

    order = [
        (begin_h, 2),
        (outer_loaded,),
        (run, inner_factors, 0, 6),
        (run, inner_factors, 6, 12),
        (run, inner_factors, 12, 18),
        (run, inner_factors, 18, 24),
        (arrived, [b_p1o]),
        (stage_1, 0, 0),
        (run, outer_h, 21, 24),
        (go, [b_ho]),
        (run, outer_h, 18, 21),
        (stage_1, 0, 1),
        (run, outer_h, 15, 18),
        (run, outer_h, 12, 15),
        (stage_1, 0, 2),
        (stage_2, 0, 0),
        (run, outer_h, 9, 12),
        (run, outer_h, 6, 9),
        (run, outer_h, 3, 6),
        (stage_2, 0, 1),
        (run, outer_h, 0, 3),
        (go, [b_p2]),
        (stage_2, 0, 2),
        (stage_3, 0, 0),
        (stage_3, 0, 1),
        (stage_3, 0, 2),
        (stage_4, 0, 0),
        (stage_4, 0, 1),
        (stage_4, 0, 2),
        (stage_5, 0, 1),
        (stage_5, 0, 0),
        (begin_e, 1),
        (stage_5, 0, 2),
        (layer_below,),
        (begin_e, 0),
        (begin_e, 2),
        (run, last_inner_row, 0, LAYERS),
        (outer_borders,),
        (run, outer_e, 0, 2),
        (run, outer_e, 2, 4),
        (run, outer_e, 4, 6),
        (stage_1, 1, 1),
        (run, outer_e, 6, 8),
        (run, outer_e, 8, 10),
        (stage_1, 1, 0),
        (run, outer_e, 10, 12),
        (run, outer_e, 12, 14),
        (stage_1, 1, 2),
        (stage_2, 1, 1),
        (run, outer_e, 14, 16),
        (run, outer_e, 16, 18),
        (stage_2, 1, 0),
        (run, outer_e, 18, 20),
        (run, outer_e, 20, 22),
        (run, outer_e, 22, 24),
        (stage_2, 1, 2),
        (stage_3, 1, 1),
        (stage_3, 1, 0),
        (stage_3, 1, 2),
        (stage_4, 1, 1),
        (stage_4, 1, 0),
        (stage_4, 1, 2),
        (drain,),
        (stage_5, 1, 1),
        (stage_5, 1, 2),
        (stage_5, 1, 0),
    ]
    for step, *what in order:
        step(*what)

    drain()
    for a in range(2):

        @pl.when(pair[a] == 3)
        def _():
            for d in d_up(a):
                d.wait_send()


def local(er, ea, eh, mr, mp, mz, material, permittivity, conductivity, mode_cutoff):
    base, phase = basis_tables()
    anywhere = pl.BlockSpec(memory_space=pltpu.HBM)
    vmem = pl.BlockSpec(memory_space=pltpu.VMEM)

    def scratch(*shape, dtype=F32):
        return pltpu.VMEM(shape, dtype)

    field = (LAYERS, NR, WIDTH)
    outer = (LAYERS, OUT, WIDTH)
    held = (
        scratch(LAYERS + 1, 2, OUT + 8, WIDTH),
        scratch(*outer),
        scratch(*outer),
        scratch(*outer),
        scratch(*outer),
        scratch(2, LAYERS + 1, 4, 16, WIDTH),
        scratch(2, LAYERS, 3, 16, WIDTH),
    )
    step = pl.pallas_call(
        kernel,
        out_shape=held,
        in_specs=[anywhere] * 12,
        out_specs=tuple([vmem] * 7),
        scratch_shapes=[
            scratch(LAYERS + 1, NR, WIDTH),
            scratch(LAYERS + 1, NR + 8, WIDTH),
            scratch(LAYERS, NR + 8, WIDTH),
            scratch(*field),
            scratch(*field),
            scratch(*field),
            scratch(*field, dtype=jnp.int32),
            pltpu.SMEM((NMAT,), F32),
            pltpu.SMEM((NMAT,), F32),
            pltpu.SMEM((NF,), jnp.int32),
            scratch(*base.shape),
            scratch(*phase.shape),
            scratch(9, NR, 128),
            scratch(2, NMAT, 8, 128),
            scratch(NF, 256),
            scratch(2, 2, 640, 256, dtype=BF16),
            scratch(NR, 128),
            scratch(OUT, 128),
            scratch(5, NF, 128),
            scratch(OUT, 128),
            scratch(OUT, 128),
            scratch(2, 2, LAYERS, 3, 16, 128),
            scratch(2, CHUNKS, 2, 3, HELD, 3, 16, 128),
            scratch(2, CHUNKS, 2, HELD, 3, 16, 256),
            scratch(2, CHUNKS, 2, HELD, 3, 8, 256),
            scratch(2, CHUNKS, 2, HELD, 3, 8, 256),
            scratch(2, CHUNKS, 2, HELD, 3, 8, 256),
            scratch(2, CHUNKS, 2, HELD, 3, 16, 256),
            scratch(CHUNKS, 2, 3, HELD, 4, 16, 128),
            scratch(CHUNKS, 2, 3, HELD, 3, 16, 128),
            scratch(LAYERS, 2, NF, 128),
            pltpu.SemaphoreType.DMA((19,)),
            pltpu.SemaphoreType.DMA((2 * CHUNKS, NSTAGE)),
            pltpu.SemaphoreType.DMA((2 * CHUNKS, NSTAGE)),
            pltpu.SemaphoreType.DMA((NBORDER,)),
            pltpu.SemaphoreType.DMA((NBORDER,)),
        ],
        compiler_params=pltpu.CompilerParams(
            collective_id=0, has_side_effects=True, vmem_limit_bytes=40 * 1024 * 1024
        ),
        name="yee_step",
    )
    operands = (
        er, ea, eh, mr, mp, mz, material, permittivity, conductivity, mode_cutoff,
        jnp.asarray(base), jnp.asarray(phase),
    )
    return rows_out(*step(*(pltpu.with_memory_space_constraint(x, pltpu.HBM) for x in operands)))


def rows_out(ho, o_hz, o_er, o_ea, o_eh, rz1, rz2):
    vmem = pl.BlockSpec(memory_space=pltpu.VMEM)
    hbm = pl.BlockSpec(memory_space=pltpu.HBM)
    return pl.pallas_call(
        write_kernel,
        out_shape=tuple(jax.ShapeDtypeStruct((LAYERS, NR, WIDTH), F32) for _ in range(6)),
        in_specs=[vmem] * 7,
        out_specs=tuple([hbm] * 6),
        scratch_shapes=[pltpu.SemaphoreType.DMA((40,))],
        compiler_params=pltpu.CompilerParams(vmem_limit_bytes=1024 * 1024),
        name="write_fields",
    )(ho, o_hz, o_er, o_ea, o_eh, rz1, rz2)

def write_kernel(ho, o_hz, o_er, o_ea, o_eh, rz1, rz2, w_er, w_ea, w_eh, w_hr, w_hp, w_hz, sem):
    copies = []

    def add(src, dst):
        copies.append(pltpu.make_async_copy(src, dst, sem.at[len(copies)]))

    for o, w in ((o_hz, w_hz), (o_er, w_er), (o_ea, w_ea), (o_eh, w_eh)):
        add(o, w.at[:, NF:NR])
    for n, w in ((0, w_hr), (1, w_hp)):
        add(ho.at[1 : LAYERS + 1, n, 8:104], w.at[:, NF:NR])
    for a in range(2):
        rows = slice(16 * a, 16 * a + 16)
        for n, w in enumerate((w_hr, w_hp, w_hz)):
            add(rz1.at[a, 1 : LAYERS + 1, n], w.at[:, rows])
        for n, w in enumerate((w_er, w_ea, w_eh)):
            add(rz2.at[a, :, n], w.at[:, rows])
    for d in copies:
        d.start()
    for d in copies:
        d.wait()


def solution(mesh):
    field = P("gz", None, "phi")
    return jax.shard_map(
        local,
        mesh=mesh,
        in_specs=(field,) * 7 + (P(),) * 3,
        out_specs=(field,) * 6,
        check_vma=False,
    )
```

```python
import math

import jax
import jax.numpy as jnp
import numpy as np
from jax import lax
from jax.experimental import pallas as pl
from jax.experimental.pallas import tpu as pltpu
from jax.sharding import PartitionSpec as P

KMAX = 128
NF = 32
NMAT = 8
NPHI = 2048
NR = 128
OUT = NR - NF
LAYERS = 24
WIDTH = 128
CHUNKS = 6
PER_CHUNK = LAYERS // CHUNKS
HELD = PER_CHUNK // 4
HALO_R = 32

inner_radius = 64.0
dt = 0.2
dphi = 2.0 * math.pi / NPHI
MESH = pl.DeviceIdType.MESH
F32 = jnp.float32
BF16 = jnp.bfloat16

C_DT_RN, C_UP, C_HERE, C_DT_RC, C_RC, C_KEEP_PREV, C_P, C_Q, C_RN = range(9)
ST_Q, ST_2, ST_C, ST_Z = 0, 6, 8, 9
NSTAGE = 15
B_P1O, B_ER, B_EA, B_P2, B_HO, B_P1Q, B_HI = 0, 1, 2, 3, 4, 5, 10
NBORDER = 20


def basis_tables():
    j = np.arange(WIDTH + 8, dtype=np.float64)[:, None]
    j[WIDTH:] = -1.0
    m = np.arange(KMAX, dtype=np.float64)[None, :]
    a = 2.0 * np.pi * j * m / NPHI
    base = np.stack([np.cos(a), np.sin(a)])
    turn = 2.0 * np.pi * ((np.arange(16)[:, None] * WIDTH * np.arange(KMAX)[None, :]) % NPHI) / NPHI
    phase = np.stack([np.cos(turn), np.sin(turn)])
    return base.astype(np.float32), phase.astype(np.float32)


def split(x):
    hi = x.astype(BF16)
    lo = (x - hi.astype(F32)).astype(BF16)
    return hi, lo


def dot3(x, b_hi, b_lo, dims):
    hi, lo = split(x)

    def dot(a, b):
        return lax.dot_general(a, b, (dims, ((), ())), preferred_element_type=F32)

    m = x.shape[0]
    high = dot(jnp.concatenate([hi, lo], axis=0), b_hi)
    return high[0:m] + high[m : 2 * m] + dot(hi, b_lo)


def kernel(
    er_h, ea_h, eh_h, mr_h, mp_h, mz_h, mat_h, perm_h, cond_h, cut_h, base_h, phase_h,
    ho, o_hz, o_er, o_ea, o_eh, rz1, rz2,
    er, ea, eh, mr, mp, mz, mat,
    perm, cond, cut, base, phase,
    coef, ktab, wts, tab,
    p1s, p1r, p1q, p2s, p2r,
    g, rq, s, r2, u, ru, v1, v2, ki,
    in_sem, send, recv, bsend, brecv,
):
    phi = lax.axis_index("phi")
    gz = lax.axis_index("gz")
    q = phi % 2
    z = (phi // 2) % 4
    hi_bit = z // 2
    low_bit = z % 2
    gray = (hi_bit + low_bit) % 2
    sib = phi + 1 - 2 * q
    half = (phi // 8) * 8
    dev_z1 = half + (z + 1 - 2 * low_bit) * 2 + q
    dev_z3 = half + (3 - z) * 2 + q
    sib_z1 = dev_z1 + 1 - 2 * q
    sib_z3 = dev_z3 + 1 - 2 * q
    dev_y = (phi + 8) % 16
    nxt = (phi + 1) % 16
    prv = (phi + 15) % 16
    up = (gz + 1) % 8
    down = (gz + 7) % 8
    first_bit = (gray, hi_bit)
    first_dev = ((dev_z1, sib_z1), (dev_z3, sib_z3))
    second_dev = (dev_z3, dev_z1)
    pair = tuple(2 * q + b for b in first_bit)

    lane = lax.broadcasted_iota(jnp.int32, (1, 128), 1)

    small = [
        pltpu.make_async_copy(src, dst, in_sem.at[14 + n])
        for n, (src, dst) in enumerate(
            [(base_h, base), (phase_h, phase), (perm_h, perm), (cond_h, cond), (cut_h, cut)]
        )
    ]
    loads = []
    RI = 40
    for n, (src, dst) in enumerate(
        [(eh_h, eh), (er_h, er.at[0:LAYERS]), (ea_h, ea.at[0:LAYERS]), (mr_h, mr), (mp_h, mp), (mz_h, mz), (mat_h, mat)]
    ):
        inner = pltpu.make_async_copy(src.at[:, 0:RI], dst.at[:, 0:RI], in_sem.at[2 * n])
        outer = pltpu.make_async_copy(src.at[:, RI:NR], dst.at[:, RI:NR], in_sem.at[2 * n + 1])
        loads.append((inner, outer))

    barrier = pltpu.get_barrier_semaphore()
    quads = (sib, dev_z1, sib_z1, dev_z3, sib_z3)
    for d in quads + (dev_y, nxt, prv):
        pl.semaphore_signal(barrier, inc=1, device_id={"phi": d}, device_id_type=MESH)
    for slab in (up, down):
        for d in quads + (phi,):
            pl.semaphore_signal(barrier, inc=1, device_id={"phi": d, "gz": slab}, device_id_type=MESH)
    for inner, _ in loads[0:2]:
        inner.start()
    for d in small:
        d.start()
    for inner, _ in loads[2:]:
        inner.start()
    for _, outer in loads:
        outer.start()

    p1s[...] = jnp.zeros_like(p1s)
    p2s[...] = jnp.zeros_like(p2s)

    def pack_first(lo, hi):
        def body(k, _):
            a = pltpu.roll(eh[k, lo:hi], k, 1)
            b = pltpu.roll(er[k, lo:hi], HALO_R + k, 1)
            p1s[lo:hi] = jnp.where(lane == k, a, jnp.where(lane == HALO_R + k, b, p1s[lo:hi]))
            return 0

        lax.fori_loop(0, LAYERS, body, 0)

    def clear(k, _):
        eh[k, NR : NR + 8] = jnp.zeros((8, 128), F32)
        ea[k, NR : NR + 8] = jnp.zeros((8, 128), F32)
        return 0

    lax.fori_loop(0, LAYERS, clear, 0)
    row = lax.broadcasted_iota(jnp.int32, (NR, 128), 0)
    rn = inner_radius + row.astype(F32)
    rc = rn + 0.5
    inv_rn = 1.0 / rn
    inv_rc = 1.0 / rc
    first = row == 0
    coef[C_DT_RN] = (dt / dphi) * inv_rn
    coef[C_UP] = dt * (rn + 1.0) * inv_rc
    coef[C_HERE] = dt * rn * inv_rc
    coef[C_DT_RC] = (dt / dphi) * inv_rc
    coef[C_RC] = (1.0 / dphi) * inv_rc
    coef[C_KEEP_PREV] = jnp.where(first, 0.0, 1.0)
    coef[C_P] = rc * inv_rn
    coef[C_Q] = jnp.where(first, 0.0, (rc - 1.0) * inv_rn)
    coef[C_RN] = (1.0 / dphi) * inv_rn
    def border(src, dst, n, dev, arrival=None):
        return pltpu.make_async_remote_copy(
            src_ref=src, dst_ref=dst, send_sem=bsend.at[n], recv_sem=brecv.at[n if arrival is None else arrival],
            device_id=dev, device_id_type=MESH,
        )

    b_er = border(er_h.at[0], er.at[LAYERS], B_ER, {"gz": down})
    b_ea = border(ea_h.at[0], ea.at[LAYERS, 0:NR], B_EA, {"gz": down})
    b_p1q = [border(p1s.at[0:NF], p1q.at[n], B_P1Q + n, {"phi": d}) for n, d in enumerate(quads)]
    b_p1o = border(p1s.at[NF:NR], p1r, B_P1O, {"phi": prv})
    b_p2 = border(p2s, p2r, B_P2, {"phi": nxt})
    b_ho = border(ho.at[LAYERS, :, 8:104], ho.at[0, :, 8:104], B_HO, {"gz": up})

    def magnetic(k, lo, hi):
        def ahead(x, n):
            edge = 0.0 if lo == 0 else pltpu.roll(p1r[...], 127 - n, 1)
            return jnp.where(lane == 127, edge, pltpu.roll(x, 127, 1)) - x

        e_h = eh[k, lo:hi]
        e_r = er[k, lo:hi]
        e_a = ea[k, lo:hi]
        hr = mr[k, lo:hi] - coef[C_DT_RN, lo:hi] * ahead(e_h, k) + dt * (ea[k + 1, lo:hi] - e_a)
        hp = mp[k, lo:hi] - dt * ((er[k + 1, lo:hi] - e_r) - (eh[k, lo + 1 : hi + 1] - e_h))
        hz = (
            mz[k, lo:hi]
            - (coef[C_UP, lo:hi] * ea[k, lo + 1 : hi + 1] - coef[C_HERE, lo:hi] * e_a)
            + coef[C_DT_RC, lo:hi] * ahead(e_r, HALO_R + k)
        )
        return hr, hp, hz

    def factors(k, lo, hi):
        kind = mat[k, lo:hi]
        keep = jnp.broadcast_to(ktab[0, 0, 0:1], kind.shape)
        drive = jnp.broadcast_to(ktab[1, 0, 0:1], kind.shape)
        for number in range(1, NMAT):
            here = kind == number
            keep = jnp.where(here, ktab[0, number, 0:1], keep)
            drive = jnp.where(here, ktab[1, number, 0:1], drive)
        return keep, drive

    def move(f, c, stage, src, dst, dev):
        n = f * CHUNKS + c
        return pltpu.make_async_remote_copy(
            src_ref=src, dst_ref=dst, send_sem=send.at[n, stage], recv_sem=recv.at[n, stage],
            device_id={"phi": dev}, device_id_type=MESH,
        )

    def d_q(f, c):
        out = []
        for a in range(2):
            b = first_bit[a]
            owners = (2 * q + 1 - b, 2 * (1 - q) + 1 - b, 2 * (1 - q) + b)
            devs = first_dev[a] + (sib,)
            slots = (1, 2, 0)
            for n in range(3):
                src = g.at[f, a, pl.ds(PER_CHUNK * c + HELD * owners[n], HELD)]
                out.append(move(f, c, ST_Q + 3 * a + n, src, rq.at[f, c, a, slots[n]], devs[n]))
        return out

    def d_2(f, c, sets=(0, 1)):
        return [
            move(f, c, ST_2 + a, s.at[f, c, a], r2.at[f, c, a], second_dev[a])
            for a in sets
        ]

    def d_c(f, c):
        return [move(f, c, ST_C, u.at[f, c], ru.at[f, c], dev_y)]

    def d_z(f, c, sets=(0, 1)):
        out = []
        for a in sets:
            devs = first_dev[a] + (sib,)
            slots = (1, 2, 0)
            for n in range(3):
                if f == 0:
                    src, dst = v1.at[c, a, slots[n]], rz1.at[a, pl.ds(1 + PER_CHUNK * c + HELD * pair[a], HELD)]
                else:
                    src, dst = v2.at[c, a, slots[n]], rz2.at[a, pl.ds(PER_CHUNK * c + HELD * pair[a], HELD)]
                out.append(move(f, c, ST_Z + 3 * a + n, src, dst, devs[n]))
        return out

    def d_up(a):
        devs = (sib,) + first_dev[a] + (phi,)
        srcs = [v1.at[CHUNKS - 1, a, n, HELD - 1, 0:2] for n in range(3)] + [rz1.at[a, LAYERS, 0:2]]
        return [
            border(srcs[n], rz1.at[a, 0, 0:2], B_HI + 4 * a + n, {"phi": devs[n], "gz": up}, B_HI + a)
            for n in range(4)
        ]

    started = []

    def go(copies):
        for d in copies:
            d.start()
            started.append(d)

    def arrived(copies):
        for d in copies:
            d.wait_recv()

    def stage_1(f, c):
        arrived(d_q(f, c))
        for a in range(2):
            k = PER_CHUNK * c + HELD * pair[a]
            own = g[f, a, pl.ds(k, HELD)].reshape(48 * HELD, 128)
            parts = [own] + [rq[f, c, a, n].reshape(48 * HELD, 128) for n in range(3)]
            width = 512
            if f == 0:
                rows = slice(16 * a, 16 * a + 16)
                tiles = [p1s[rows]] + [p1q[n, rows] for n in ((0, 1, 2), (0, 3, 4))[a]]
                extra = []
                for l in range(HELD):
                    height = jnp.zeros((16, 128), F32)
                    radial = jnp.zeros((16, 128), F32)
                    for m in range(4):
                        here = lane == 32 * m
                        height = jnp.where(here, pltpu.roll(tiles[m], (32 * m + 128 - k - l) % 128, 1), height)
                        radial = jnp.where(here, pltpu.roll(tiles[m], (32 * m + 128 - HALO_R - k - l) % 128, 1), radial)
                    extra += [-coef[C_DT_RN, rows] * height, jnp.zeros((16, 128), F32), coef[C_DT_RC, rows] * radial]
                parts.append(jnp.concatenate(extra, axis=0))
                width = 640
            x = jnp.concatenate(parts, axis=1)
            s[f, c, a] = dot3(x, tab[0, a, 0:width], tab[1, a, 0:width], ((1,), (0,))).reshape(HELD, 3, 16, 256)
            go(d_2(f, c, (a,)))

    def stage_2(f, c):
        arrived(d_2(f, c))
        for a in range(2):
            u[f, c, a] = s[f, c, a] + r2[f, c, a]
        go(d_c(f, c))

    def stage_4(f, c):
        arrived(d_c(f, c))
        for a in range(2):
            w = wts[16 * a : 16 * a + 16]
            x = ((u[f, c, a] + ru[f, c, a]) * w[None, None]).reshape(48 * HELD, 256)
            k = PER_CHUNK * c + HELD * pair[a]
            if f == 0:
                y = dot3(x, tab[0, a], tab[1, a], ((1,), (1,))).reshape(HELD, 3, 16, 640)
                before = jnp.where(lane % 32 == 0, y[:, 0, :, 512:640], y[:, 2, :, 512:640])
                for n in range(3):
                    v1[c, a, n, :, 0:3] = y[..., 128 * n + 128 : 128 * n + 256]
                    v1[c, a, n, :, 3] = before
                go(d_z(f, c, (a,)))
                rz1[a, pl.ds(1 + k, HELD), 0:3] = y[..., 0:128]
                rz1[a, pl.ds(1 + k, HELD), 3] = before
                if c == CHUNKS - 1:

                    @pl.when(pair[a] == 3)
                    def _():
                        for d in d_up(a):
                            d.start()

            else:
                y = dot3(x, tab[0, a, 0:512], tab[1, a, 0:512], ((1,), (1,))).reshape(HELD, 3, 16, 512)
                for n in range(3):
                    v2[c, a, n] = y[..., 128 * n + 128 : 128 * n + 256]
                go(d_z(f, c, (a,)))
                rz2[a, pl.ds(k, HELD)] = y[..., 0:128]

    def stage_5(f, c):
        arrived(d_z(f, c))

    def put(f, k, n, x):
        g[f, 0, k, n] = x[0:16]
        g[f, 1, k, n] = x[16:32]

    def update_h(lo, hi):
        def body(k, _):
            for n, x in enumerate(magnetic(k, 0, NF)):
                put(0, k, n, x)
            return 0

        lax.fori_loop(lo, hi, body, 0)

    below = jnp.where(gz == 0, 0.0, 1.0)

    def electric_inner(k, _):
        owner = (k % PER_CHUNK) // HELD

        def get(place, n):
            return jnp.concatenate([rz1[0, place, n], rz1[1, place, n]], axis=0)

        hr, hp, hz = (get(k + 1, n) for n in range(3))
        hr_below, hp_below = get(k, 0), get(k, 1)
        own_q, own_b = owner // 2, owner % 2
        off_q = own_q + q - 2 * own_q * q
        marks = []
        for a in range(2):
            off_b = own_b + first_bit[a] - 2 * own_b * first_bit[a]
            marks.append(32 * (off_q + 2 * off_b))

        def behind(x, n):
            edge = jnp.concatenate(
                [pltpu.roll(rz1[a, k + 1, 3], (128 - marks[a] - n) % 128, 1) for a in range(2)], axis=0
            )
            return x - jnp.where(lane == 0, edge, pltpu.roll(x, 1, 1))

        keep, drive = ki[k, 0], ki[k, 1]
        back = pltpu.roll(hp, 1, 0)
        put(1, k, 0, keep * er[k, 0:NF] + drive * (coef[C_RC, 0:NF] * behind(hz, 1) - (hp - hp_below)))
        put(
            1, k, 1,
            keep * ea[k, 0:NF] + drive * ((hr - hr_below) - (hp - coef[C_KEEP_PREV, 0:NF] * back)),
        )
        put(
            1, k, 2,
            keep * eh[k, 0:NF]
            + drive * (coef[C_P, 0:NF] * hp - coef[C_Q, 0:NF] * back - coef[C_RN, 0:NF] * behind(hr, 0)),
        )
        return 0

    def begin_e(c):
        lax.fori_loop(PER_CHUNK * c, PER_CHUNK * c + PER_CHUNK, electric_inner, 0)
        go(d_q(1, c))

    def inner_factors(k, _):
        keep, drive = factors(k, 0, NF)
        ki[k, 0] = keep
        ki[k, 1] = drive
        return 0

    def basis():
        for d in small:
            d.wait()

        for kind in range(2):
            for place, who in enumerate((phi, sib) + first_dev[kind]):
                pc = phase[0, pl.ds(who, 1), :]
                ps = phase[1, pl.ds(who, 1), :]
                if kind == 1 and place < 2:
                    tab[:, 1, place * 128 : place * 128 + 128] = tab[:, 0, place * 128 : place * 128 + 128]
                else:
                    for part, m in ((0, base[0, 0:128] * pc - base[1, 0:128] * ps), (1, base[1, 0:128] * pc + base[0, 0:128] * ps)):
                        h, l = split(m)
                        tab[0, kind, place * 128 : place * 128 + 128, part * 128 : part * 128 + 128] = h
                        tab[1, kind, place * 128 : place * 128 + 128, part * 128 : part * 128 + 128] = l
                bc, bs = base[0, 128:129], base[1, 128:129]
                lo_row = 512 + place * 32
                for part, m in ((0, bc * pc - bs * ps), (1, bs * pc + bc * ps)):
                    h, l = split(jnp.broadcast_to(m, (32, 128)))
                    tab[0, kind, lo_row : lo_row + 32, part * 128 : part * 128 + 128] = h
                    tab[1, kind, lo_row : lo_row + 32, part * 128 : part * 128 + 128] = l


    def tables():
        for number in range(NMAT):
            eps = jnp.full((8, 128), perm[number], F32)
            sig = jnp.full((8, 128), cond[number], F32)
            loss = sig * dt / (2.0 * eps)
            ktab[0, number] = (1.0 - loss) / (1.0 + loss)
            ktab[1, number] = dt / (eps * (1.0 + loss))
        mode = lax.broadcasted_iota(jnp.int32, (NF, 128), 1)
        wrow = lax.broadcasted_iota(jnp.int32, (NF, 128), 0)
        cuts = jnp.zeros((NF, 128), jnp.int32)
        for number in range(NF):
            cuts = jnp.where(wrow == number, cut[number], cuts)
        weight = jnp.where(mode == 0, 1.0 / NPHI, 2.0 / NPHI)
        weight = jnp.where(mode <= cuts, weight, 0.0)
        wts[:, 0:128] = weight
        wts[:, 128:256] = weight

    def outer_h(k, _):
        hr, hp, hz = magnetic(k, NF, NR)
        ho[k + 1, 0, 8:104] = hr
        ho[k + 1, 1, 8:104] = hp
        o_hz[k] = hz
        p2s[...] = jnp.where(
            lane == k,
            pltpu.roll(hr, k + 1, 1),
            jnp.where(lane == HALO_R + k, pltpu.roll(hz, HALO_R + k + 1, 1), p2s[...]),
        )
        return 0

    def last_inner_row(k, _):
        ho[k + 1, 1, 0:8] = rz1[1, k + 1, 1, 8:16]
        return 0

    def outer_e(k, _):
        hr, hp, hz = ho[k + 1, 0, 8:104], ho[k + 1, 1, 8:104], o_hz[k]
        back = ho[k + 1, 1, 7:103]
        keep, drive = factors(k, NF, NR)

        def behind(x, n):
            return x - jnp.where(lane == 0, pltpu.roll(p2r[...], (128 - n) % 128, 1), pltpu.roll(x, 1, 1))

        o_er[k] = keep * er[k, NF:NR] + drive * (coef[C_RC, NF:NR] * behind(hz, HALO_R + k) - (hp - ho[k, 1, 8:104]))
        o_ea[k] = keep * ea[k, NF:NR] + drive * ((hr - ho[k, 0, 8:104]) - (hp - back))
        o_eh[k] = keep * eh[k, NF:NR] + drive * (
            coef[C_P, NF:NR] * hp - coef[C_Q, NF:NR] * back - coef[C_RN, NF:NR] * behind(hr, k)
        )
        return 0

    def run(body, lo, hi):
        lax.fori_loop(lo, hi, body, 0)

    def outer_loaded():
        for n in range(7):
            loads[n][1].wait()
        pack_first(NF, NR)
        go([b_p1o])

    def layer_above():
        arrived([b_er, b_ea])
        above = jnp.where(gz == 7, 0.0, 1.0)
        er[LAYERS] = er[LAYERS] * above
        ea[LAYERS, 0:NR] = ea[LAYERS, 0:NR] * above

    def begin_h(c):
        update_h(PER_CHUNK * c, PER_CHUNK * c + PER_CHUNK)
        go(d_q(0, c))

    def layer_below():
        for a in range(2):
            arrived(d_up(a)[0:1])
            rz1[a, 0, 0:2] = rz1[a, 0, 0:2] * below

    def outer_borders():
        arrived([b_p2, b_ho])
        ho[0, :, 8:104] = ho[0, :, 8:104] * below

    def drain():
        while started:
            started.pop().wait_send()

    for n in range(6):
        loads[n][0].wait()
    pack_first(0, NF)
    update_h(0, PER_CHUNK)
    pl.semaphore_wait(barrier, 20)
    go([b_er, b_ea] + d_q(0, 0) + b_p1q)
    if CHUNKS > 2:
        begin_h(1)
    basis()
    layer_above()
    if CHUNKS == 2:
        begin_h(1)
    tables()
    loads[6][0].wait()
    arrived(b_p1q)

    order = [
        (outer_loaded,),
        (run, inner_factors, 0, 6),
        (run, inner_factors, 6, 12),
        (run, inner_factors, 12, 18),
        (begin_h, 2),
        (stage_1, 0, 0),
        (begin_h, 3),
        (stage_1, 0, 1),
        (run, inner_factors, 18, 24),
        (arrived, [b_p1o]),
        (run, outer_h, 21, 24),
        (go, [b_ho]),
        (run, outer_h, 18, 21),
        (run, outer_h, 15, 18),
        (run, outer_h, 12, 15),
        (begin_h, 4),
        (stage_1, 0, 2),
        (stage_2, 0, 0),
        (run, outer_h, 9, 12),
        (begin_h, 5),
        (stage_1, 0, 3),
        (stage_2, 0, 1),
        (run, outer_h, 6, 9),
        (run, outer_h, 3, 6),
        (stage_1, 0, 4),
        (stage_2, 0, 2),
        (run, outer_h, 0, 3),
        (go, [b_p2]),
        (stage_4, 0, 0),
        (stage_1, 0, 5),
        (stage_2, 0, 3),
        (stage_4, 0, 1),
        (stage_2, 0, 4),
        (stage_4, 0, 2),
        (stage_2, 0, 5),
        (stage_4, 0, 3),
        (stage_5, 0, 1),
        (stage_5, 0, 0),
        (begin_e, 1),
        (stage_4, 0, 4),
        (stage_5, 0, 2),
        (begin_e, 2),
        (stage_4, 0, 5),
        (stage_5, 0, 3),
        (begin_e, 3),
        (stage_1, 1, 1),
        (stage_5, 0, 4),
        (begin_e, 4),
        (stage_1, 1, 2),
        (stage_5, 0, 5),
        (layer_below,),
        (begin_e, 0),
        (begin_e, 5),
        (run, last_inner_row, 0, LAYERS),
        (stage_1, 1, 3),
        (stage_2, 1, 1),
        (outer_borders,),
        (run, outer_e, 0, 2),
        (run, outer_e, 2, 4),
        (stage_1, 1, 4),
        (stage_2, 1, 2),
        (run, outer_e, 4, 6),
        (run, outer_e, 6, 8),
        (stage_1, 1, 0),
        (run, outer_e, 8, 10),
        (stage_1, 1, 5),
        (stage_4, 1, 1),
        (stage_2, 1, 3),
        (stage_2, 1, 4),
        (run, outer_e, 10, 12),
        (stage_4, 1, 2),
        (stage_2, 1, 0),
        (run, outer_e, 12, 14),
        (run, outer_e, 14, 16),
        (stage_2, 1, 5),
        (run, outer_e, 16, 18),
        (run, outer_e, 18, 20),
        (run, outer_e, 20, 22),
        (stage_4, 1, 3),
        (run, outer_e, 22, 24),
        (stage_4, 1, 4),
        (stage_4, 1, 0),
        (stage_4, 1, 5),
        (drain,),
        (stage_5, 1, 1),
        (stage_5, 1, 2),
        (stage_5, 1, 3),
        (stage_5, 1, 4),
        (stage_5, 1, 5),
        (stage_5, 1, 0),
    ]
    for step, *what in order:
        step(*what)

    drain()
    for a in range(2):

        @pl.when(pair[a] == 3)
        def _():
            for d in d_up(a):
                d.wait_send()


def local(er, ea, eh, mr, mp, mz, material, permittivity, conductivity, mode_cutoff):
    base, phase = basis_tables()
    anywhere = pl.BlockSpec(memory_space=pltpu.HBM)
    vmem = pl.BlockSpec(memory_space=pltpu.VMEM)

    def scratch(*shape, dtype=F32):
        return pltpu.VMEM(shape, dtype)

    field = (LAYERS, NR, WIDTH)
    outer = (LAYERS, OUT, WIDTH)
    held = (
        scratch(LAYERS + 1, 2, OUT + 8, WIDTH),
        scratch(*outer),
        scratch(*outer),
        scratch(*outer),
        scratch(*outer),
        scratch(2, LAYERS + 1, 4, 16, WIDTH),
        scratch(2, LAYERS, 3, 16, WIDTH),
    )
    step = pl.pallas_call(
        kernel,
        out_shape=held,
        in_specs=[anywhere] * 12,
        out_specs=tuple([vmem] * 7),
        scratch_shapes=[
            scratch(LAYERS + 1, NR, WIDTH),
            scratch(LAYERS + 1, NR + 8, WIDTH),
            scratch(LAYERS, NR + 8, WIDTH),
            scratch(*field),
            scratch(*field),
            scratch(*field),
            scratch(*field, dtype=jnp.int32),
            pltpu.SMEM((NMAT,), F32),
            pltpu.SMEM((NMAT,), F32),
            pltpu.SMEM((NF,), jnp.int32),
            scratch(*base.shape),
            scratch(*phase.shape),
            scratch(9, NR, 128),
            scratch(2, NMAT, 8, 128),
            scratch(NF, 256),
            scratch(2, 2, 640, 256, dtype=BF16),
            scratch(NR, 128),
            scratch(OUT, 128),
            scratch(5, NF, 128),
            scratch(OUT, 128),
            scratch(OUT, 128),
            scratch(2, 2, LAYERS, 3, 16, 128),
            scratch(2, CHUNKS, 2, 3, HELD, 3, 16, 128),
            scratch(2, CHUNKS, 2, HELD, 3, 16, 256),
            scratch(2, CHUNKS, 2, HELD, 3, 16, 256),
            scratch(2, CHUNKS, 2, HELD, 3, 16, 256),
            scratch(2, CHUNKS, 2, HELD, 3, 16, 256),
            scratch(CHUNKS, 2, 3, HELD, 4, 16, 128),
            scratch(CHUNKS, 2, 3, HELD, 3, 16, 128),
            scratch(LAYERS, 2, NF, 128),
            pltpu.SemaphoreType.DMA((19,)),
            pltpu.SemaphoreType.DMA((2 * CHUNKS, NSTAGE)),
            pltpu.SemaphoreType.DMA((2 * CHUNKS, NSTAGE)),
            pltpu.SemaphoreType.DMA((NBORDER,)),
            pltpu.SemaphoreType.DMA((NBORDER,)),
        ],
        compiler_params=pltpu.CompilerParams(
            collective_id=0, has_side_effects=True, vmem_limit_bytes=40 * 1024 * 1024
        ),
        name="yee_step",
    )
    operands = (
        er, ea, eh, mr, mp, mz, material, permittivity, conductivity, mode_cutoff,
        jnp.asarray(base), jnp.asarray(phase),
    )
    return rows_out(*step(*(pltpu.with_memory_space_constraint(x, pltpu.HBM) for x in operands)))


def rows_out(ho, o_hz, o_er, o_ea, o_eh, rz1, rz2):
    vmem = pl.BlockSpec(memory_space=pltpu.VMEM)
    hbm = pl.BlockSpec(memory_space=pltpu.HBM)
    return pl.pallas_call(
        write_kernel,
        out_shape=tuple(jax.ShapeDtypeStruct((LAYERS, NR, WIDTH), F32) for _ in range(6)),
        in_specs=[vmem] * 7,
        out_specs=tuple([hbm] * 6),
        scratch_shapes=[pltpu.SemaphoreType.DMA((40,))],
        compiler_params=pltpu.CompilerParams(vmem_limit_bytes=1024 * 1024),
        name="write_fields",
    )(ho, o_hz, o_er, o_ea, o_eh, rz1, rz2)

def write_kernel(ho, o_hz, o_er, o_ea, o_eh, rz1, rz2, w_er, w_ea, w_eh, w_hr, w_hp, w_hz, sem):
    copies = []

    def add(src, dst):
        copies.append(pltpu.make_async_copy(src, dst, sem.at[len(copies)]))

    for o, w in ((o_hz, w_hz), (o_er, w_er), (o_ea, w_ea), (o_eh, w_eh)):
        add(o, w.at[:, NF:NR])
    for n, w in ((0, w_hr), (1, w_hp)):
        add(ho.at[1 : LAYERS + 1, n, 8:104], w.at[:, NF:NR])
    for a in range(2):
        rows = slice(16 * a, 16 * a + 16)
        for n, w in enumerate((w_hr, w_hp, w_hz)):
            add(rz1.at[a, 1 : LAYERS + 1, n], w.at[:, rows])
        for n, w in enumerate((w_er, w_ea, w_eh)):
            add(rz2.at[a, :, n], w.at[:, rows])
    for d in copies:
        d.start()
    for d in copies:
        d.wait()


def solution(mesh):
    field = P("gz", None, "phi")
    return jax.shard_map(
        local,
        mesh=mesh,
        in_specs=(field,) * 7 + (P(),) * 3,
        out_specs=(field,) * 6,
        check_vma=False,
    )
```

```python
import math

import jax
import jax.numpy as jnp
import numpy as np
from jax import lax
from jax.experimental import pallas as pl
from jax.experimental.pallas import tpu as pltpu
from jax.sharding import PartitionSpec as P

KMAX = 128
NF = 32
NMAT = 8
NPHI = 2048
NR = 128
OUT = NR - NF
LAYERS = 24
WIDTH = 128
CHUNKS = 6
PER_CHUNK = LAYERS // CHUNKS
HELD = PER_CHUNK // 4
HALO_R = 32

inner_radius = 64.0
dt = 0.2
dphi = 2.0 * math.pi / NPHI
MESH = pl.DeviceIdType.MESH
F32 = jnp.float32
BF16 = jnp.bfloat16

C_DT_RN, C_UP, C_HERE, C_DT_RC, C_RC, C_KEEP_PREV, C_P, C_Q, C_RN = range(9)
ST_Q, ST_2, ST_C, ST_Z = 0, 6, 8, 9
NSTAGE = 15
B_P1O, B_ER, B_EA, B_P2, B_HO, B_P1Q, B_HI = 0, 1, 2, 3, 4, 5, 10
NBORDER = 20


def basis_tables():
    j = np.arange(WIDTH + 8, dtype=np.float64)[:, None]
    j[WIDTH:] = -1.0
    m = np.arange(KMAX, dtype=np.float64)[None, :]
    a = 2.0 * np.pi * j * m / NPHI
    base = np.stack([np.cos(a), np.sin(a)])
    turn = 2.0 * np.pi * ((np.arange(16)[:, None] * WIDTH * np.arange(KMAX)[None, :]) % NPHI) / NPHI
    phase = np.stack([np.cos(turn), np.sin(turn)])
    return base.astype(np.float32), phase.astype(np.float32)


def split(x):
    hi = x.astype(BF16)
    lo = (x - hi.astype(F32)).astype(BF16)
    return hi, lo


def dot3(x, b_hi, b_lo, dims):
    hi, lo = split(x)

    def dot(a, b):
        return lax.dot_general(a, b, (dims, ((), ())), preferred_element_type=F32)

    m = x.shape[0]
    high = dot(jnp.concatenate([hi, lo], axis=0), b_hi)
    return high[0:m] + high[m : 2 * m] + dot(hi, b_lo)


def kernel(
    er_h, ea_h, eh_h, mr_h, mp_h, mz_h, mat_h, perm_h, cond_h, cut_h, base_h, phase_h,
    ho, o_hz, o_er, o_ea, o_eh, rz1, rz2,
    er, ea, eh, mr, mp, mz, mat,
    perm, cond, cut, base, phase,
    coef, ktab, wts, tab,
    p1s, p1r, p1q, p2s, p2r,
    g, rq, s, r2, u, ru, v1, v2, ki,
    in_sem, send, recv, bsend, brecv,
):
    phi = lax.axis_index("phi")
    gz = lax.axis_index("gz")
    q = phi % 2
    z = (phi // 2) % 4
    hi_bit = z // 2
    low_bit = z % 2
    gray = (hi_bit + low_bit) % 2
    sib = phi + 1 - 2 * q
    half = (phi // 8) * 8
    dev_z1 = half + (z + 1 - 2 * low_bit) * 2 + q
    dev_z3 = half + (3 - z) * 2 + q
    sib_z1 = dev_z1 + 1 - 2 * q
    sib_z3 = dev_z3 + 1 - 2 * q
    dev_y = (phi + 8) % 16
    nxt = (phi + 1) % 16
    prv = (phi + 15) % 16
    up = (gz + 1) % 8
    down = (gz + 7) % 8
    first_bit = (gray, hi_bit)
    first_dev = ((dev_z1, sib_z1), (dev_z3, sib_z3))
    second_dev = (dev_z3, dev_z1)
    pair = tuple(2 * q + b for b in first_bit)

    lane = lax.broadcasted_iota(jnp.int32, (1, 128), 1)

    small = [
        pltpu.make_async_copy(src, dst, in_sem.at[14 + n])
        for n, (src, dst) in enumerate(
            [(base_h, base), (phase_h, phase), (perm_h, perm), (cond_h, cond), (cut_h, cut)]
        )
    ]
    loads = []
    RI = 40
    for n, (src, dst) in enumerate(
        [(eh_h, eh), (er_h, er.at[0:LAYERS]), (ea_h, ea.at[0:LAYERS]), (mr_h, mr), (mp_h, mp), (mz_h, mz), (mat_h, mat)]
    ):
        inner = pltpu.make_async_copy(src.at[:, 0:RI], dst.at[:, 0:RI], in_sem.at[2 * n])
        outer = pltpu.make_async_copy(src.at[:, RI:NR], dst.at[:, RI:NR], in_sem.at[2 * n + 1])
        loads.append((inner, outer))

    barrier = pltpu.get_barrier_semaphore()
    quads = (sib, dev_z1, sib_z1, dev_z3, sib_z3)
    for d in quads + (dev_y, nxt, prv):
        pl.semaphore_signal(barrier, inc=1, device_id={"phi": d}, device_id_type=MESH)
    for slab in (up, down):
        for d in quads + (phi,):
            pl.semaphore_signal(barrier, inc=1, device_id={"phi": d, "gz": slab}, device_id_type=MESH)
    for inner, _ in loads[0:2]:
        inner.start()
    for d in small:
        d.start()
    for inner, _ in loads[2:]:
        inner.start()
    for _, outer in loads:
        outer.start()

    p1s[...] = jnp.zeros_like(p1s)
    p2s[...] = jnp.zeros_like(p2s)

    def pack_first(lo, hi):
        def body(k, _):
            a = pltpu.roll(eh[k, lo:hi], k, 1)
            b = pltpu.roll(er[k, lo:hi], HALO_R + k, 1)
            p1s[lo:hi] = jnp.where(lane == k, a, jnp.where(lane == HALO_R + k, b, p1s[lo:hi]))
            return 0

        lax.fori_loop(0, LAYERS, body, 0)

    def clear(k, _):
        eh[k, NR : NR + 8] = jnp.zeros((8, 128), F32)
        ea[k, NR : NR + 8] = jnp.zeros((8, 128), F32)
        return 0

    lax.fori_loop(0, LAYERS, clear, 0)
    row = lax.broadcasted_iota(jnp.int32, (NR, 128), 0)
    rn = inner_radius + row.astype(F32)
    rc = rn + 0.5
    inv_rn = 1.0 / rn
    inv_rc = 1.0 / rc
    first = row == 0
    coef[C_DT_RN] = (dt / dphi) * inv_rn
    coef[C_UP] = dt * (rn + 1.0) * inv_rc
    coef[C_HERE] = dt * rn * inv_rc
    coef[C_DT_RC] = (dt / dphi) * inv_rc
    coef[C_RC] = (1.0 / dphi) * inv_rc
    coef[C_KEEP_PREV] = jnp.where(first, 0.0, 1.0)
    coef[C_P] = rc * inv_rn
    coef[C_Q] = jnp.where(first, 0.0, (rc - 1.0) * inv_rn)
    coef[C_RN] = (1.0 / dphi) * inv_rn
    def border(src, dst, n, dev, arrival=None):
        return pltpu.make_async_remote_copy(
            src_ref=src, dst_ref=dst, send_sem=bsend.at[n], recv_sem=brecv.at[n if arrival is None else arrival],
            device_id=dev, device_id_type=MESH,
        )

    b_er = border(er_h.at[0], er.at[LAYERS], B_ER, {"gz": down})
    b_ea = border(ea_h.at[0], ea.at[LAYERS, 0:NR], B_EA, {"gz": down})
    b_p1q = [border(p1s.at[0:NF], p1q.at[n], B_P1Q + n, {"phi": d}) for n, d in enumerate(quads)]
    b_p1o = border(p1s.at[NF:NR], p1r, B_P1O, {"phi": prv})
    b_p2 = border(p2s, p2r, B_P2, {"phi": nxt})
    b_ho = border(ho.at[LAYERS, :, 8:104], ho.at[0, :, 8:104], B_HO, {"gz": up})

    def magnetic(k, lo, hi):
        def ahead(x, n):
            edge = 0.0 if lo == 0 else pltpu.roll(p1r[...], 127 - n, 1)
            return jnp.where(lane == 127, edge, pltpu.roll(x, 127, 1)) - x

        e_h = eh[k, lo:hi]
        e_r = er[k, lo:hi]
        e_a = ea[k, lo:hi]
        hr = mr[k, lo:hi] - coef[C_DT_RN, lo:hi] * ahead(e_h, k) + dt * (ea[k + 1, lo:hi] - e_a)
        hp = mp[k, lo:hi] - dt * ((er[k + 1, lo:hi] - e_r) - (eh[k, lo + 1 : hi + 1] - e_h))
        hz = (
            mz[k, lo:hi]
            - (coef[C_UP, lo:hi] * ea[k, lo + 1 : hi + 1] - coef[C_HERE, lo:hi] * e_a)
            + coef[C_DT_RC, lo:hi] * ahead(e_r, HALO_R + k)
        )
        return hr, hp, hz

    def factors(k, lo, hi):
        kind = mat[k, lo:hi]
        keep = jnp.broadcast_to(ktab[0, 0, 0:1], kind.shape)
        drive = jnp.broadcast_to(ktab[1, 0, 0:1], kind.shape)
        for number in range(1, NMAT):
            here = kind == number
            keep = jnp.where(here, ktab[0, number, 0:1], keep)
            drive = jnp.where(here, ktab[1, number, 0:1], drive)
        return keep, drive

    def move(f, c, stage, src, dst, dev):
        n = f * CHUNKS + c
        return pltpu.make_async_remote_copy(
            src_ref=src, dst_ref=dst, send_sem=send.at[n, stage], recv_sem=recv.at[n, stage],
            device_id={"phi": dev}, device_id_type=MESH,
        )

    def d_q(f, c):
        out = []
        for a in range(2):
            b = first_bit[a]
            owners = (2 * q + 1 - b, 2 * (1 - q) + 1 - b, 2 * (1 - q) + b)
            devs = first_dev[a] + (sib,)
            slots = (1, 2, 0)
            for n in range(3):
                src = g.at[f, a, pl.ds(PER_CHUNK * c + HELD * owners[n], HELD)]
                out.append(move(f, c, ST_Q + 3 * a + n, src, rq.at[f, c, a, slots[n]], devs[n]))
        return out

    def d_2(f, c, sets=(0, 1)):
        return [
            move(f, c, ST_2 + a, s.at[f, c, a], r2.at[f, c, a], second_dev[a])
            for a in sets
        ]

    def d_c(f, c):
        return [move(f, c, ST_C, u.at[f, c], ru.at[f, c], dev_y)]

    def d_z(f, c, sets=(0, 1)):
        out = []
        for a in sets:
            devs = first_dev[a] + (sib,)
            slots = (1, 2, 0)
            for n in range(3):
                if f == 0:
                    src, dst = v1.at[c, a, slots[n]], rz1.at[a, pl.ds(1 + PER_CHUNK * c + HELD * pair[a], HELD)]
                else:
                    src, dst = v2.at[c, a, slots[n]], rz2.at[a, pl.ds(PER_CHUNK * c + HELD * pair[a], HELD)]
                out.append(move(f, c, ST_Z + 3 * a + n, src, dst, devs[n]))
        return out

    def d_up(a):
        devs = (sib,) + first_dev[a] + (phi,)
        srcs = [v1.at[CHUNKS - 1, a, n, HELD - 1, 0:2] for n in range(3)] + [rz1.at[a, LAYERS, 0:2]]
        return [
            border(srcs[n], rz1.at[a, 0, 0:2], B_HI + 4 * a + n, {"phi": devs[n], "gz": up}, B_HI + a)
            for n in range(4)
        ]

    started = []

    def go(copies):
        for d in copies:
            d.start()
            started.append(d)

    def arrived(copies):
        for d in copies:
            d.wait_recv()

    def stage_1(f, c):
        arrived(d_q(f, c))
        for a in range(2):
            k = PER_CHUNK * c + HELD * pair[a]
            own = g[f, a, pl.ds(k, HELD)].reshape(48 * HELD, 128)
            parts = [own] + [rq[f, c, a, n].reshape(48 * HELD, 128) for n in range(3)]
            width = 512
            if f == 0:
                rows = slice(16 * a, 16 * a + 16)
                tiles = [p1s[rows]] + [p1q[n, rows] for n in ((0, 1, 2), (0, 3, 4))[a]]
                extra = []
                for l in range(HELD):
                    height = jnp.zeros((16, 128), F32)
                    radial = jnp.zeros((16, 128), F32)
                    for m in range(4):
                        here = lane == 32 * m
                        height = jnp.where(here, pltpu.roll(tiles[m], (32 * m + 128 - k - l) % 128, 1), height)
                        radial = jnp.where(here, pltpu.roll(tiles[m], (32 * m + 128 - HALO_R - k - l) % 128, 1), radial)
                    extra += [-coef[C_DT_RN, rows] * height, jnp.zeros((16, 128), F32), coef[C_DT_RC, rows] * radial]
                parts.append(jnp.concatenate(extra, axis=0))
                width = 640
            x = jnp.concatenate(parts, axis=1)
            s[f, c, a] = dot3(x, tab[0, a, 0:width], tab[1, a, 0:width], ((1,), (0,))).reshape(HELD, 3, 16, 256)
            go(d_2(f, c, (a,)))

    def stage_2(f, c):
        arrived(d_2(f, c))
        for a in range(2):
            u[f, c, a] = s[f, c, a] + r2[f, c, a]
        go(d_c(f, c))

    def stage_4(f, c):
        arrived(d_c(f, c))
        for a in range(2):
            w = wts[16 * a : 16 * a + 16]
            x = ((u[f, c, a] + ru[f, c, a]) * w[None, None]).reshape(48 * HELD, 256)
            k = PER_CHUNK * c + HELD * pair[a]
            if f == 0:
                y = dot3(x, tab[0, a], tab[1, a], ((1,), (1,))).reshape(HELD, 3, 16, 640)
                before = jnp.where(lane % 32 == 0, y[:, 0, :, 512:640], y[:, 2, :, 512:640])
                for n in range(3):
                    v1[c, a, n, :, 0:3] = y[..., 128 * n + 128 : 128 * n + 256]
                    v1[c, a, n, :, 3] = before
                go(d_z(f, c, (a,)))
                rz1[a, pl.ds(1 + k, HELD), 0:3] = y[..., 0:128]
                rz1[a, pl.ds(1 + k, HELD), 3] = before
                if c == CHUNKS - 1:

                    @pl.when(pair[a] == 3)
                    def _():
                        for d in d_up(a):
                            d.start()

            else:
                y = dot3(x, tab[0, a, 0:512], tab[1, a, 0:512], ((1,), (1,))).reshape(HELD, 3, 16, 512)
                for n in range(3):
                    v2[c, a, n] = y[..., 128 * n + 128 : 128 * n + 256]
                go(d_z(f, c, (a,)))
                rz2[a, pl.ds(k, HELD)] = y[..., 0:128]

    def stage_5(f, c):
        arrived(d_z(f, c))

    def put(f, k, n, x):
        g[f, 0, k, n] = x[0:16]
        g[f, 1, k, n] = x[16:32]

    def update_h(lo, hi):
        def body(k, _):
            for n, x in enumerate(magnetic(k, 0, NF)):
                put(0, k, n, x)
            return 0

        lax.fori_loop(lo, hi, body, 0)

    below = jnp.where(gz == 0, 0.0, 1.0)

    def electric_inner(k, _):
        owner = (k % PER_CHUNK) // HELD

        def get(place, n):
            return jnp.concatenate([rz1[0, place, n], rz1[1, place, n]], axis=0)

        hr, hp, hz = (get(k + 1, n) for n in range(3))
        hr_below, hp_below = get(k, 0), get(k, 1)
        own_q, own_b = owner // 2, owner % 2
        off_q = own_q + q - 2 * own_q * q
        marks = []
        for a in range(2):
            off_b = own_b + first_bit[a] - 2 * own_b * first_bit[a]
            marks.append(32 * (off_q + 2 * off_b))

        def behind(x, n):
            edge = jnp.concatenate(
                [pltpu.roll(rz1[a, k + 1, 3], (128 - marks[a] - n) % 128, 1) for a in range(2)], axis=0
            )
            return x - jnp.where(lane == 0, edge, pltpu.roll(x, 1, 1))

        keep, drive = ki[k, 0], ki[k, 1]
        back = pltpu.roll(hp, 1, 0)
        put(1, k, 0, keep * er[k, 0:NF] + drive * (coef[C_RC, 0:NF] * behind(hz, 1) - (hp - hp_below)))
        put(
            1, k, 1,
            keep * ea[k, 0:NF] + drive * ((hr - hr_below) - (hp - coef[C_KEEP_PREV, 0:NF] * back)),
        )
        put(
            1, k, 2,
            keep * eh[k, 0:NF]
            + drive * (coef[C_P, 0:NF] * hp - coef[C_Q, 0:NF] * back - coef[C_RN, 0:NF] * behind(hr, 0)),
        )
        return 0

    def begin_e(c):
        lax.fori_loop(PER_CHUNK * c, PER_CHUNK * c + PER_CHUNK, electric_inner, 0)
        go(d_q(1, c))

    def inner_factors(k, _):
        keep, drive = factors(k, 0, NF)
        ki[k, 0] = keep
        ki[k, 1] = drive
        return 0

    def basis():
        for d in small:
            d.wait()

        for kind in range(2):
            for place, who in enumerate((phi, sib) + first_dev[kind]):
                pc = phase[0, pl.ds(who, 1), :]
                ps = phase[1, pl.ds(who, 1), :]
                if kind == 1 and place < 2:
                    tab[:, 1, place * 128 : place * 128 + 128] = tab[:, 0, place * 128 : place * 128 + 128]
                else:
                    for part, m in ((0, base[0, 0:128] * pc - base[1, 0:128] * ps), (1, base[1, 0:128] * pc + base[0, 0:128] * ps)):
                        h, l = split(m)
                        tab[0, kind, place * 128 : place * 128 + 128, part * 128 : part * 128 + 128] = h
                        tab[1, kind, place * 128 : place * 128 + 128, part * 128 : part * 128 + 128] = l
                bc, bs = base[0, 128:129], base[1, 128:129]
                lo_row = 512 + place * 32
                for part, m in ((0, bc * pc - bs * ps), (1, bs * pc + bc * ps)):
                    h, l = split(jnp.broadcast_to(m, (32, 128)))
                    tab[0, kind, lo_row : lo_row + 32, part * 128 : part * 128 + 128] = h
                    tab[1, kind, lo_row : lo_row + 32, part * 128 : part * 128 + 128] = l


    def tables():
        for number in range(NMAT):
            eps = jnp.full((8, 128), perm[number], F32)
            sig = jnp.full((8, 128), cond[number], F32)
            loss = sig * dt / (2.0 * eps)
            ktab[0, number] = (1.0 - loss) / (1.0 + loss)
            ktab[1, number] = dt / (eps * (1.0 + loss))
        mode = lax.broadcasted_iota(jnp.int32, (NF, 128), 1)
        wrow = lax.broadcasted_iota(jnp.int32, (NF, 128), 0)
        cuts = jnp.zeros((NF, 128), jnp.int32)
        for number in range(NF):
            cuts = jnp.where(wrow == number, cut[number], cuts)
        weight = jnp.where(mode == 0, 1.0 / NPHI, 2.0 / NPHI)
        weight = jnp.where(mode <= cuts, weight, 0.0)
        wts[:, 0:128] = weight
        wts[:, 128:256] = weight

    def outer_h(k, _):
        hr, hp, hz = magnetic(k, NF, NR)
        ho[k + 1, 0, 8:104] = hr
        ho[k + 1, 1, 8:104] = hp
        o_hz[k] = hz
        p2s[...] = jnp.where(
            lane == k,
            pltpu.roll(hr, k + 1, 1),
            jnp.where(lane == HALO_R + k, pltpu.roll(hz, HALO_R + k + 1, 1), p2s[...]),
        )
        return 0

    def last_inner_row(k, _):
        ho[k + 1, 1, 0:8] = rz1[1, k + 1, 1, 8:16]
        return 0

    def outer_e(k, _):
        hr, hp, hz = ho[k + 1, 0, 8:104], ho[k + 1, 1, 8:104], o_hz[k]
        back = ho[k + 1, 1, 7:103]
        keep, drive = factors(k, NF, NR)

        def behind(x, n):
            return x - jnp.where(lane == 0, pltpu.roll(p2r[...], (128 - n) % 128, 1), pltpu.roll(x, 1, 1))

        o_er[k] = keep * er[k, NF:NR] + drive * (coef[C_RC, NF:NR] * behind(hz, HALO_R + k) - (hp - ho[k, 1, 8:104]))
        o_ea[k] = keep * ea[k, NF:NR] + drive * ((hr - ho[k, 0, 8:104]) - (hp - back))
        o_eh[k] = keep * eh[k, NF:NR] + drive * (
            coef[C_P, NF:NR] * hp - coef[C_Q, NF:NR] * back - coef[C_RN, NF:NR] * behind(hr, k)
        )
        return 0

    def run(body, lo, hi):
        lax.fori_loop(lo, hi, body, 0)

    def outer_loaded():
        for n in range(7):
            loads[n][1].wait()
        pack_first(NF, NR)
        go([b_p1o])

    def layer_above():
        arrived([b_er, b_ea])
        above = jnp.where(gz == 7, 0.0, 1.0)
        er[LAYERS] = er[LAYERS] * above
        ea[LAYERS, 0:NR] = ea[LAYERS, 0:NR] * above

    def begin_h(c):
        update_h(PER_CHUNK * c, PER_CHUNK * c + PER_CHUNK)
        go(d_q(0, c))

    def layer_below():
        for a in range(2):
            arrived(d_up(a)[0:1])
            rz1[a, 0, 0:2] = rz1[a, 0, 0:2] * below

    def outer_borders():
        arrived([b_p2, b_ho])
        ho[0, :, 8:104] = ho[0, :, 8:104] * below

    def drain():
        while started:
            started.pop().wait_send()

    for n in range(6):
        loads[n][0].wait()
    pack_first(0, NF)
    update_h(0, PER_CHUNK)
    pl.semaphore_wait(barrier, 20)
    go([b_er, b_ea] + d_q(0, 0) + b_p1q)
    if CHUNKS > 2:
        begin_h(1)
    basis()
    layer_above()
    if CHUNKS == 2:
        begin_h(1)
    tables()
    loads[6][0].wait()
    arrived(b_p1q)

    order = [
        (outer_loaded,),
        (run, inner_factors, 0, 6),
        (begin_h, 2),
        (stage_1, 0, 0),
        (begin_h, 3),
        (stage_1, 0, 1),
        (run, inner_factors, 6, 12),
        (run, inner_factors, 12, 18),
        (run, inner_factors, 18, 24),
        (arrived, [b_p1o]),
        (run, outer_h, 21, 24),
        (go, [b_ho]),
        (run, outer_h, 18, 21),
        (begin_h, 4),
        (stage_1, 0, 2),
        (stage_2, 0, 0),
        (run, outer_h, 15, 18),
        (run, outer_h, 12, 15),
        (begin_h, 5),
        (stage_1, 0, 3),
        (stage_2, 0, 1),
        (run, outer_h, 9, 12),
        (stage_1, 0, 4),
        (run, outer_h, 6, 9),
        (stage_2, 0, 2),
        (stage_4, 0, 0),
        (stage_1, 0, 5),
        (run, outer_h, 3, 6),
        (stage_2, 0, 3),
        (stage_4, 0, 1),
        (stage_2, 0, 4),
        (run, outer_h, 0, 3),
        (go, [b_p2]),
        (stage_4, 0, 2),
        (stage_2, 0, 5),
        (stage_4, 0, 3),
        (stage_5, 0, 1),
        (stage_5, 0, 0),
        (begin_e, 1),
        (stage_4, 0, 4),
        (stage_5, 0, 2),
        (begin_e, 2),
        (stage_4, 0, 5),
        (stage_5, 0, 3),
        (begin_e, 3),
        (stage_1, 1, 1),
        (stage_5, 0, 4),
        (begin_e, 4),
        (stage_1, 1, 2),
        (stage_5, 0, 5),
        (layer_below,),
        (begin_e, 0),
        (begin_e, 5),
        (run, last_inner_row, 0, LAYERS),
        (stage_1, 1, 3),
        (outer_borders,),
        (stage_2, 1, 1),
        (run, outer_e, 0, 2),
        (run, outer_e, 2, 4),
        (stage_1, 1, 4),
        (stage_2, 1, 2),
        (run, outer_e, 4, 6),
        (run, outer_e, 6, 8),
        (stage_1, 1, 0),
        (stage_1, 1, 5),
        (stage_4, 1, 1),
        (stage_2, 1, 3),
        (run, outer_e, 8, 10),
        (stage_2, 1, 4),
        (stage_4, 1, 2),
        (stage_2, 1, 0),
        (run, outer_e, 10, 12),
        (run, outer_e, 12, 14),
        (stage_2, 1, 5),
        (run, outer_e, 14, 16),
        (run, outer_e, 16, 18),
        (stage_4, 1, 3),
        (run, outer_e, 18, 20),
        (stage_4, 1, 4),
        (run, outer_e, 20, 22),
        (stage_4, 1, 0),
        (run, outer_e, 22, 24),
        (stage_4, 1, 5),
        (drain,),
        (stage_5, 1, 1),
        (stage_5, 1, 2),
        (stage_5, 1, 3),
        (stage_5, 1, 4),
        (stage_5, 1, 5),
        (stage_5, 1, 0),
    ]
    for step, *what in order:
        step(*what)

    drain()
    for a in range(2):

        @pl.when(pair[a] == 3)
        def _():
            for d in d_up(a):
                d.wait_send()


def local(er, ea, eh, mr, mp, mz, material, permittivity, conductivity, mode_cutoff):
    base, phase = basis_tables()
    anywhere = pl.BlockSpec(memory_space=pltpu.HBM)
    vmem = pl.BlockSpec(memory_space=pltpu.VMEM)

    def scratch(*shape, dtype=F32):
        return pltpu.VMEM(shape, dtype)

    field = (LAYERS, NR, WIDTH)
    outer = (LAYERS, OUT, WIDTH)
    held = (
        scratch(LAYERS + 1, 2, OUT + 8, WIDTH),
        scratch(*outer),
        scratch(*outer),
        scratch(*outer),
        scratch(*outer),
        scratch(2, LAYERS + 1, 4, 16, WIDTH),
        scratch(2, LAYERS, 3, 16, WIDTH),
    )
    step = pl.pallas_call(
        kernel,
        out_shape=held,
        in_specs=[anywhere] * 12,
        out_specs=tuple([vmem] * 7),
        scratch_shapes=[
            scratch(LAYERS + 1, NR, WIDTH),
            scratch(LAYERS + 1, NR + 8, WIDTH),
            scratch(LAYERS, NR + 8, WIDTH),
            scratch(*field),
            scratch(*field),
            scratch(*field),
            scratch(*field, dtype=jnp.int32),
            pltpu.SMEM((NMAT,), F32),
            pltpu.SMEM((NMAT,), F32),
            pltpu.SMEM((NF,), jnp.int32),
            scratch(*base.shape),
            scratch(*phase.shape),
            scratch(9, NR, 128),
            scratch(2, NMAT, 8, 128),
            scratch(NF, 256),
            scratch(2, 2, 640, 256, dtype=BF16),
            scratch(NR, 128),
            scratch(OUT, 128),
            scratch(5, NF, 128),
            scratch(OUT, 128),
            scratch(OUT, 128),
            scratch(2, 2, LAYERS, 3, 16, 128),
            scratch(2, CHUNKS, 2, 3, HELD, 3, 16, 128),
            scratch(2, CHUNKS, 2, HELD, 3, 16, 256),
            scratch(2, CHUNKS, 2, HELD, 3, 16, 256),
            scratch(2, CHUNKS, 2, HELD, 3, 16, 256),
            scratch(2, CHUNKS, 2, HELD, 3, 16, 256),
            scratch(CHUNKS, 2, 3, HELD, 4, 16, 128),
            scratch(CHUNKS, 2, 3, HELD, 3, 16, 128),
            scratch(LAYERS, 2, NF, 128),
            pltpu.SemaphoreType.DMA((19,)),
            pltpu.SemaphoreType.DMA((2 * CHUNKS, NSTAGE)),
            pltpu.SemaphoreType.DMA((2 * CHUNKS, NSTAGE)),
            pltpu.SemaphoreType.DMA((NBORDER,)),
            pltpu.SemaphoreType.DMA((NBORDER,)),
        ],
        compiler_params=pltpu.CompilerParams(
            collective_id=0, has_side_effects=True, vmem_limit_bytes=40 * 1024 * 1024
        ),
        name="yee_step",
    )
    operands = (
        er, ea, eh, mr, mp, mz, material, permittivity, conductivity, mode_cutoff,
        jnp.asarray(base), jnp.asarray(phase),
    )
    return rows_out(*step(*(pltpu.with_memory_space_constraint(x, pltpu.HBM) for x in operands)))


def rows_out(ho, o_hz, o_er, o_ea, o_eh, rz1, rz2):
    vmem = pl.BlockSpec(memory_space=pltpu.VMEM)
    hbm = pl.BlockSpec(memory_space=pltpu.HBM)
    return pl.pallas_call(
        write_kernel,
        out_shape=tuple(jax.ShapeDtypeStruct((LAYERS, NR, WIDTH), F32) for _ in range(6)),
        in_specs=[vmem] * 7,
        out_specs=tuple([hbm] * 6),
        scratch_shapes=[pltpu.SemaphoreType.DMA((40,))],
        compiler_params=pltpu.CompilerParams(vmem_limit_bytes=1024 * 1024),
        name="write_fields",
    )(ho, o_hz, o_er, o_ea, o_eh, rz1, rz2)

def write_kernel(ho, o_hz, o_er, o_ea, o_eh, rz1, rz2, w_er, w_ea, w_eh, w_hr, w_hp, w_hz, sem):
    copies = []

    def add(src, dst):
        copies.append(pltpu.make_async_copy(src, dst, sem.at[len(copies)]))

    for o, w in ((o_hz, w_hz), (o_er, w_er), (o_ea, w_ea), (o_eh, w_eh)):
        add(o, w.at[:, NF:NR])
    for n, w in ((0, w_hr), (1, w_hp)):
        add(ho.at[1 : LAYERS + 1, n, 8:104], w.at[:, NF:NR])
    for a in range(2):
        rows = slice(16 * a, 16 * a + 16)
        for n, w in enumerate((w_hr, w_hp, w_hz)):
            add(rz1.at[a, 1 : LAYERS + 1, n], w.at[:, rows])
        for n, w in enumerate((w_er, w_ea, w_eh)):
            add(rz2.at[a, :, n], w.at[:, rows])
    for d in copies:
        d.start()
    for d in copies:
        d.wait()


def solution(mesh):
    field = P("gz", None, "phi")
    return jax.shard_map(
        local,
        mesh=mesh,
        in_specs=(field,) * 7 + (P(),) * 3,
        out_specs=(field,) * 6,
        check_vma=False,
    )
```
